128 devices in a mesh: ctx: 64 (over y_hi, x, z, core), ch: 2 (over y_lo).
Axes of the slice: x: 4, y: 4 (y_hi: 2, y_lo: 2; y = y_hi * 2 + y_lo), z: 4, core: 2. Of those that a mesh axis runs over, the one named last changes fastest.
Arguments:
- qkv: bfloat16 [3, 32768, 4096], P(None, 'ctx', 'ch'), may hold values from -6 to 6
- short_filter: float32 [3, 3, 4096], P(None, None, 'ch'), may hold values from -3 to 3
- long_filter: bfloat16 [2048, 4096], P(None, 'ch'), may hold values from -0.125 to 0.125
- skip: float32 [4096], P('ch'), may hold values from -1 to 1
- shard_doc: int32 [64], replicated, may hold values from 0 to 15, as said below
- live: int32 [64], replicated, may hold values from 1 to 512
Outputs:
- filtered: bfloat16 [2, 2048, 32768], P(None, 'ctx', 'ch')
The draws below stay inside these ranges and needn't reach their ends.
Inputs may be any that keep to these rules, and one draw needn't show every extreme that they name: `shard_doc`: documents occupy whole consecutive shards in order; each document spans 1 to 16 shards and one spans exactly 16. Read only for a shard that ends a document; its tokens at offsets from live on are padding.
All inputs are finite; a program needn't handle non-finite values.
Results may differ from the reference program's by a relative error of at most 0.012.
Values may be sent and summed in bfloat16 or wider, within the bound.
A program may use at most 256 MiB of HBM per device.

```python
import jax
import jax.numpy as jnp

D = 4096
TOK_DEV = 512
FILT = 2048
SHARDS = 64
TOKENS = 32768
DOCS = 16
DOCMOST = 16
N_CH = 2


def draw_shard_doc(key, part):
    order_key = jax.random.fold_in(key, 11)
    place_key = jax.random.fold_in(key, 23)
    others = DOCS - 1
    rest = SHARDS - DOCMOST
    base_len = 1 + (rest - others) // others
    surplus = (rest - others) % others
    ranks = jax.random.permutation(order_key, others).astype(jnp.int32)
    small_lens = base_len + (ranks < surplus).astype(jnp.int32)
    where_big = jax.random.randint(place_key, (), 0, DOCS, dtype=jnp.int32)
    slots = jnp.arange(DOCS, dtype=jnp.int32)
    before = jnp.clip(slots, 0, others - 1)
    after = jnp.clip(slots - 1, 0, others - 1)
    all_lens = jnp.where(slots < where_big, small_lens[before], jnp.where(slots == where_big, DOCMOST, small_lens[after]))
    ends = jnp.cumsum(all_lens).astype(jnp.int32)
    shard_ids = jnp.arange(SHARDS, dtype=jnp.int32)
    return jnp.sum((shard_ids[:, None] >= ends[None, :]).astype(jnp.int32), axis=1).astype(jnp.int32)


def set_ends(result, own_key, low, high):
    index_at = [jax.random.randint(jax.random.fold_in(own_key, axis), (), 0, length) for axis, length in enumerate(result.shape)]
    widest = result.shape.index(max(result.shape))
    beside = index_at[:widest] + [(index_at[widest] + 1) % result.shape[widest]] + index_at[widest + 1:]
    return result.at[tuple(index_at)].set(low).at[tuple(beside)].set(high)


def steps_of(stream_key, extent, shards, low, largest):
    level, own = 1.0, jax.random.fold_in(stream_key, 6)
    for dim, parts in shards:
        draws = jnp.exp(jax.random.uniform(jax.random.fold_in(own, dim), (parts,), jnp.float32, low / len(shards), largest / len(shards)))
        level = level * jnp.repeat(draws, extent[dim] // parts).reshape([-1 if axis == dim else 1 for axis in range(len(extent))])
    return level


def bell_draw(key, shape, width, limit, pieces=(), kind=jnp.bfloat16):
    factor_of = steps_of(key, shape, pieces, -0.22, 0.18) if pieces else 1.0
    values = jax.random.normal(key, shape, jnp.float32) * width * factor_of
    return jnp.minimum(jnp.maximum(values, -limit), limit).astype(kind)


def setup_inputs(seed: int = 0) -> dict:
    key_list = jax.random.split(jax.random.key(seed), 7)
    qkv = bell_draw(key_list[0], (3, TOKENS, D), 1.0, 6.0, ((1, 64), (2, 2)))
    short_filter = bell_draw(key_list[1], (3, 3, D), 0.6, 3.0, ((2, 2),), jnp.float32)
    long_filter = bell_draw(key_list[2], (FILT, D), FILT ** -0.5, 0.125, ((1, 2),))
    skip = jnp.clip(jax.random.uniform(key_list[3], (D,), jnp.float32, -1.0, 1.0) * steps_of(key_list[3], (D,), ((0, 2),), -0.4, 0.0), -1.0, 1.0)
    shard_doc = draw_shard_doc(jax.random.fold_in(key_list[6], 71), 0)
    live = set_ends(jax.random.randint(key_list[5], (SHARDS,), 1, TOK_DEV + 1), jax.random.fold_in(key_list[5], 1), 1, TOK_DEV).astype(jnp.int32)
    return dict(qkv=qkv, short_filter=short_filter, long_filter=long_filter, skip=skip, shard_doc=shard_doc, live=live)


def reference(qkv, short_filter, long_filter, skip, shard_doc, live):
    tok_rows = TOK_DEV
    spans = FILT // TOK_DEV
    shard_total = SHARDS
    offsets = jnp.arange(tok_rows, dtype=jnp.int32)
    prev_doc = jnp.concatenate([jnp.full((1,), -1, jnp.int32), shard_doc[:-1]])
    next_doc = jnp.concatenate([shard_doc[1:], jnp.full((1,), -1, jnp.int32)])
    joined = prev_doc == shard_doc
    closing = next_doc != shard_doc
    keep = (jnp.logical_not(closing)[:, None] | (offsets[None, :] < live[:, None])).astype(jnp.float32).reshape(TOKENS, 1)
    link_one = ((offsets >= 1)[None, :] | joined[:, None]).astype(jnp.float32).reshape(TOKENS, 1)
    link_two = ((offsets >= 2)[None, :] | joined[:, None]).astype(jnp.float32).reshape(TOKENS, 1)

    def short_conv(index):
        signal = qkv[index].astype(jnp.float32)
        first = jnp.concatenate([jnp.zeros((1, D), jnp.float32), signal[:-1]], axis=0) * link_one
        second = jnp.concatenate([jnp.zeros((2, D), jnp.float32), signal[:-2]], axis=0) * link_two
        return short_filter[index, 0][None, :] * signal + short_filter[index, 1][None, :] * first + short_filter[index, 2][None, :] * second

    queries = short_conv(0).astype(jnp.bfloat16)
    gated = (short_conv(1) * short_conv(2) * keep).astype(jnp.bfloat16)
    blocks = gated.astype(jnp.float32).reshape(shard_total, tok_rows, D)
    spectra = jnp.fft.rfft(blocks, n=2 * tok_rows, axis=1)
    filter_spec = jnp.fft.rfft(long_filter.astype(jnp.float32).reshape(spans, tok_rows, D), n=2 * tok_rows, axis=1)
    totals = jnp.zeros_like(spectra)
    for lag_block in range(spans):
        source_doc = jnp.concatenate([jnp.full((lag_block,), -1, jnp.int32), shard_doc[:shard_total - lag_block]])
        shifted = jnp.concatenate([jnp.zeros((lag_block, tok_rows + 1, D), spectra.dtype), spectra[:shard_total - lag_block]], axis=0)
        totals = totals + jnp.where((source_doc == shard_doc)[:, None, None], filter_spec[lag_block][None] * shifted, 0)
    conv_full = jnp.fft.irfft(totals, n=2 * tok_rows, axis=1)
    spill = jnp.concatenate([jnp.zeros((1, tok_rows, D), conv_full.dtype), conv_full[:-1, tok_rows:]], axis=0)
    spill = spill * joined.astype(conv_full.dtype)[:, None, None]
    conv = (conv_full[:, :tok_rows] + spill).reshape(TOKENS, D)
    mixed = queries.astype(jnp.float32) * (conv + skip[None, :] * gated.astype(jnp.float32)) * keep
    return mixed.astype(jnp.bfloat16).T.reshape(N_CH, D // N_CH, TOKENS)
```

```python
import functools

import jax
import jax.numpy as jnp
from jax import lax
from jax.experimental import pallas as pl
from jax.experimental.pallas import tpu as pltpu
from jax.sharding import PartitionSpec as P

MESH = pl.DeviceIdType.MESH
LANES = 128
TOK = 512
BLOCKS = TOK // LANES
RING = 32
CHUNKS = 4
HALF = 8
WIDTH = 2 * HALF
SPAN = 16
ROWS = RING * BLOCKS
LAGS = SPAN + 1
TAIL = SPAN // BLOCKS


def bordered(x, above, taps):
    place = lax.broadcasted_iota(jnp.int32, x.shape, 0)
    one = jnp.where(place == 0, above[1:2], pltpu.roll(x, 1, 0))
    two = jnp.where(place == 0, above[0:1], jnp.where(place == 1, above[1:2], pltpu.roll(x, 2, 0)))
    return taps[0:1] * x + taps[1:2] * one + taps[2:3] * two


def gate_kernel(lo_ref, hi_ref, above_lo, above_hi, taps_lo, taps_hi, keep_ref, gated_ref, query_ref):
    keep = keep_ref[...]
    flat = []
    for ref, above, taps in ((lo_ref, above_lo, taps_lo), (hi_ref, above_hi, taps_hi)):
        parts = [
            bordered(ref[a].astype(jnp.float32), above[a].astype(jnp.float32), taps[a])
            for a in range(3)
        ]
        query = parts[0].astype(jnp.bfloat16).astype(jnp.float32) * keep
        gated = parts[1] * parts[2] * keep
        flat.append((gated, query))
    for which, out_ref in enumerate((gated_ref, query_ref)):
        for block in range(BLOCKS):
            rows = slice(block * LANES, (block + 1) * LANES)
            first = flat[0][which][rows].T
            second = flat[1][which][rows].T
            for peer in range(4):
                for chunk in range(CHUNKS):
                    at = peer * 32 + chunk * HALF
                    both = jnp.concatenate([first[at : at + HALF], second[at : at + HALF]], axis=0)
                    out_ref[chunk, peer, block] = both.astype(jnp.bfloat16)


def gate_call(qkv, above, taps, keep):
    width = qkv.shape[2]
    steps = width // (2 * LANES)
    sent = jax.ShapeDtypeStruct((CHUNKS, RING, BLOCKS, WIDTH, LANES), jnp.bfloat16)
    out_spec = pl.BlockSpec((CHUNKS, 4, BLOCKS, WIDTH, LANES), lambda i: (0, i, 0, 0, 0))
    lo = lambda i: (0, 0, i)
    hi = lambda i: (0, 0, i + steps)
    return pl.pallas_call(
        gate_kernel,
        grid=(steps,),
        in_specs=[
            pl.BlockSpec((3, TOK, LANES), lo),
            pl.BlockSpec((3, TOK, LANES), hi),
            pl.BlockSpec((3, 2, LANES), lo),
            pl.BlockSpec((3, 2, LANES), hi),
            pl.BlockSpec((3, 3, LANES), lo),
            pl.BlockSpec((3, 3, LANES), hi),
            pl.BlockSpec((TOK, LANES), lambda i: (0, 0)),
        ],
        out_specs=[out_spec, out_spec],
        out_shape=[sent, sent],
        compiler_params=pltpu.CompilerParams(vmem_limit_bytes=40 * 2**20),
    )(qkv, qkv, above, above, taps, taps, keep)


def displacements():
    groups = [
        [(1, 0), (0, 1), (-1, 0), (0, -1)],
        [(1, 1), (-1, -1)],
        [(1, -1), (-1, 1)],
        [(2, 0), (0, 2)],
        [(2, 1), (1, 2), (2, -1), (-1, 2)],
        [(2, 2)],
    ]
    order = [(dx, dz, core) for core in (0, 1) for group in groups for dx, dz in group]
    return [(0, 0, 1)] + order


def fill_toeplitz(taps_ref, toep_ref, channel, slot):
    taps = taps_ref[channel]
    row = lax.broadcasted_iota(jnp.int32, (LANES, LANES), 0)
    col = lax.broadcasted_iota(jnp.int32, (LANES, LANES), 1)
    causal = col >= row
    older = jnp.zeros((LANES, LANES), jnp.bfloat16)
    for lag in range(LAGS):
        newer = jnp.zeros((LANES, LANES), jnp.bfloat16)
        if lag < SPAN:
            spread = jnp.broadcast_to(taps[lag : lag + 1], (LANES, LANES))
            newer = pltpu.roll(spread, 0, 1, stride=1, stride_axis=0).astype(jnp.bfloat16)
        toep_ref[slot, lag * LANES : (lag + 1) * LANES] = jnp.where(causal, newer, older)
        older = newer


def convolve(wide_ref, toep_ref, mask_ref, total_ref, channel, slot):
    tiles = {
        u: wide_ref[pl.ds((SPAN + u) * WIDTH + channel, 16, stride=8 * WIDTH), :].astype(jnp.bfloat16)
        for u in range(-SPAN, 8)
    }
    columns = [
        jnp.concatenate([tiles[p - lag] for p in range(8)], axis=0) * mask_ref[lag]
        for lag in range(LAGS)
    ]
    left = jnp.concatenate(columns, axis=1)
    total = jnp.dot(left, toep_ref[slot], preferred_element_type=jnp.float32)
    for p in range(8):
        total_ref[pl.ds(p * WIDTH + channel, 16, stride=8 * WIDTH), :] = total[p * 16 : (p + 1) * 16]


def exchange_kernel(
    gated_ref, query_ref, taps_ref, skip_ref, mask_ref, out_ref,
    got, edge, wide, total, ready, toep,
    send_sem, recv_sem, edge_send, edge_recv, turn_send, turn_recv,
):
    place = lax.axis_index("ctx")
    group = lax.axis_index("ch")
    half = place // RING
    ring = lax.rem(place, RING)
    x, z, core = ring // 8, lax.rem(ring // 2, 4), lax.rem(ring, 2)
    base = half * RING

    barrier = pltpu.get_barrier_semaphore()

    @pl.loop(1, RING)
    def _(k):
        peer = (base + lax.rem(ring + k, RING), group)
        pl.semaphore_signal(barrier, inc=1, device_id=peer, device_id_type=MESH)

    for other in range(2):
        @pl.when(jnp.logical_not((half == group) & (group == other)))
        def _():
            peer = (group * RING + ring, other)
            pl.semaphore_signal(barrier, inc=1, device_id=peer, device_id_type=MESH)

    @pl.when(half == 1)
    def _():
        pl.semaphore_signal(barrier, inc=1, device_id=(ring, group), device_id_type=MESH)

    expected = RING - 1 + jnp.where(half == group, 1, 2) + jnp.where(half == 0, 1, 0)
    pl.semaphore_wait(barrier, expected)

    sources = (gated_ref, query_ref)

    def send(chunk, kind):
        for dx, dz, dc in displacements():
            to = (lax.rem(x + dx + 4, 4) * 4 + lax.rem(z + dz + 4, 4)) * 2 + lax.rem(core + dc, 2)
            pltpu.make_async_remote_copy(
                src_ref=sources[kind].at[chunk, to],
                dst_ref=got.at[chunk, kind, ring],
                send_sem=send_sem.at[chunk, kind],
                recv_sem=recv_sem.at[chunk, kind],
                device_id=(base + to, group),
                device_id_type=MESH,
            ).start()
        pltpu.make_async_copy(
            sources[kind].at[chunk, ring], got.at[chunk, kind, ring], recv_sem.at[chunk, kind]
        ).start()

    def arrived(chunk, kind):
        pltpu.make_async_copy(
            sources[kind].at[chunk], got.at[chunk, kind], recv_sem.at[chunk, kind]
        ).wait()

    def edge_copy(chunk):
        return pltpu.make_async_remote_copy(
            src_ref=got.at[chunk, 0, pl.ds(RING - TAIL, TAIL)],
            dst_ref=edge.at[chunk],
            send_sem=edge_send.at[chunk],
            recv_sem=edge_recv.at[chunk],
            device_id=(RING + ring, group),
            device_id_type=MESH,
        )

    def turn_copy(chunk, part):
        return pltpu.make_async_remote_copy(
            src_ref=ready.at[chunk, part],
            dst_ref=out_ref.at[group, pl.ds(chunk * HALF, HALF)],
            send_sem=turn_send.at[chunk, part],
            recv_sem=turn_recv.at[0],
            device_id=(part * RING + ring, half),
            device_id_type=MESH,
        )

    for chunk, kind in ((0, 0), (1, 0), (0, 1), (2, 0), (1, 1), (3, 0), (2, 1), (3, 1)):
        send(chunk, kind)

    @pl.loop(0, CHUNKS)
    def _(chunk):
        arrived(chunk, 0)

        @pl.when(half == 0)
        def _():
            edge_copy(chunk).start()
            wide[pl.ds(0, SPAN * WIDTH)] = jnp.zeros((SPAN * WIDTH, LANES), jnp.float32)

        @pl.loop(0, RING)
        def _(shard):
            at = pl.multiple_of((SPAN + shard * BLOCKS) * WIDTH, 8)
            wide[pl.ds(at, BLOCKS * WIDTH)] = (
                got[chunk, 0, shard].reshape(BLOCKS * WIDTH, LANES).astype(jnp.float32)
            )

        @pl.when(half == 1)
        def _():
            edge_copy(chunk).wait_recv()
            for shard in range(TAIL):
                wide[shard * BLOCKS * WIDTH : (shard + 1) * BLOCKS * WIDTH] = (
                    edge[chunk, shard].reshape(BLOCKS * WIDTH, LANES).astype(jnp.float32)
                )

        @pl.loop(0, WIDTH // 4)
        def _(four):
            for i in range(4):
                fill_toeplitz(taps_ref, toep, chunk * WIDTH + four * 4 + i, i)
            for i in range(4):
                convolve(wide, toep, mask_ref, total, four * 4 + i, i)

        arrived(chunk, 1)
        direct = skip_ref[pl.ds(pl.multiple_of(chunk * WIDTH, WIDTH), WIDTH)]

        @pl.loop(0, RING)
        def _(shard):
            for block in range(BLOCKS):
                row = shard * BLOCKS + block
                at = pl.multiple_of(row * WIDTH, WIDTH)
                gated = got[chunk, 0, shard, block].astype(jnp.float32)
                query = got[chunk, 1, shard, block].astype(jnp.float32)
                value = (query * (total[pl.ds(at, WIDTH)] + direct * gated)).astype(jnp.bfloat16)
                to = pl.multiple_of(row * LANES, LANES)
                ready[chunk, 0, :, pl.ds(to, LANES)] = value[:HALF]
                ready[chunk, 1, :, pl.ds(to, LANES)] = value[HALF:]

        for part in range(2):
            stays = (half == group) & (half == part)

            @pl.when(stays)
            def _():
                pltpu.make_async_copy(
                    ready.at[chunk, part],
                    out_ref.at[group, pl.ds(chunk * HALF, HALF)],
                    turn_recv.at[0],
                ).start()

            @pl.when(jnp.logical_not(stays))
            def _():
                turn_copy(chunk, part).start()

    @pl.loop(0, CHUNKS)
    def _(chunk):
        for kind in range(2):
            pltpu.make_async_remote_copy(
                src_ref=sources[kind].at[chunk, pl.ds(0, RING - 1)],
                dst_ref=got.at[chunk, kind, pl.ds(0, RING - 1)],
                send_sem=send_sem.at[chunk, kind],
                recv_sem=recv_sem.at[chunk, kind],
                device_id=(place, group),
                device_id_type=MESH,
            ).wait_send()
        for part in range(2):
            @pl.when(jnp.logical_not((half == group) & (half == part)))
            def _():
                turn_copy(chunk, part).wait_send()

        @pl.when(half == 0)
        def _():
            edge_copy(chunk).wait_send()

    pltpu.make_async_copy(out_ref, out_ref, turn_recv.at[0]).wait()


def exchange_call(gated, query, taps, skip, mask, tokens):
    vmem = pl.BlockSpec(memory_space=pltpu.VMEM)
    hbm = pl.BlockSpec(memory_space=pl.ANY)
    dma = pltpu.SemaphoreType.DMA
    return pl.pallas_call(
        exchange_kernel,
        out_shape=jax.ShapeDtypeStruct((2, CHUNKS * HALF, tokens), jnp.bfloat16),
        in_specs=[hbm, hbm, vmem, vmem, vmem],
        out_specs=hbm,
        scratch_shapes=[
            pltpu.VMEM((CHUNKS, 2, RING, BLOCKS, WIDTH, LANES), jnp.bfloat16),
            pltpu.VMEM((CHUNKS, TAIL, BLOCKS, WIDTH, LANES), jnp.bfloat16),
            pltpu.VMEM(((SPAN + ROWS) * WIDTH, LANES), jnp.float32),
            pltpu.VMEM((ROWS * WIDTH, LANES), jnp.float32),
            pltpu.VMEM((CHUNKS, 2, HALF, tokens), jnp.bfloat16),
            pltpu.VMEM((4, LAGS * LANES, LANES), jnp.bfloat16),
            dma((CHUNKS, 2)),
            dma((CHUNKS, 2)),
            dma((CHUNKS,)),
            dma((CHUNKS,)),
            dma((CHUNKS, 2)),
            dma((1,)),
        ],
        compiler_params=pltpu.CompilerParams(
            collective_id=0, has_side_effects=True, vmem_limit_bytes=48 * 2**20
        ),
    )(gated, query, taps, skip, mask)


def local(qkv, short_filter, long_filter, skip, shard_doc, live):
    shards = lax.axis_size("ctx")
    here = lax.axis_index("ctx")
    half = here // RING
    ring = lax.rem(here, RING)
    spots = jnp.arange(shards, dtype=jnp.int32)
    before = jnp.concatenate([jnp.full((1,), -1, jnp.int32), shard_doc[:-1]])
    after = jnp.concatenate([shard_doc[1:], jnp.full((1,), -1, jnp.int32)])
    mine = spots == here
    joined = jnp.any(mine & (before == shard_doc))
    closing = jnp.any(mine & (after != shard_doc))
    living = jnp.sum(jnp.where(mine, live, 0))

    route = [(i, i + 1) for i in range(shards - 1)]
    above = lax.ppermute(qkv[:, TOK - 2 :, :], "ctx", route)
    above = jnp.where(joined, above, jnp.zeros_like(above))

    offsets = lax.broadcasted_iota(jnp.int32, (TOK, LANES), 0)
    keep = (jnp.logical_not(closing) | (offsets < living)).astype(jnp.float32)
    gated, query = gate_call(qkv, above, short_filter, keep)

    chosen = lax.dynamic_index_in_dim(
        long_filter.reshape(-1, 2, RING, CHUNKS, HALF), ring, axis=2, keepdims=False
    )
    taps = chosen.transpose(2, 1, 3, 0).reshape(CHUNKS * WIDTH, SPAN, LANES).astype(jnp.float32)
    direct = lax.dynamic_index_in_dim(
        skip.reshape(2, RING, CHUNKS, HALF), ring, axis=1, keepdims=False
    )
    direct = direct.transpose(1, 0, 2).reshape(CHUNKS * WIDTH, 1)
    direct = jnp.broadcast_to(direct, (CHUNKS * WIDTH, LANES))

    index = jnp.arange(ROWS, dtype=jnp.int32)
    row = (index % 16) * 8 + index // 16 + half * ROWS
    source = row[None, :] - jnp.arange(LAGS, dtype=jnp.int32)[:, None]
    opens = (before != shard_doc)[None, :] & (spots[None, :] <= spots[:, None])
    first = jnp.max(jnp.where(opens, spots[None, :], 0), axis=1) * BLOCKS
    start = jnp.sum(
        jnp.where((row // BLOCKS)[:, None] == spots[None, :], first[None, :], 0), axis=1
    )
    mask = (source >= start[None, :]).astype(jnp.bfloat16)
    mask = jnp.broadcast_to(mask[:, :, None], (LAGS, ROWS, LANES))
    return exchange_call(gated, query, taps, direct, mask, ROWS * LANES)


def solution(mesh):
    return jax.shard_map(
        local,
        mesh=mesh,
        in_specs=(P(None, "ctx", "ch"), P(None, None, "ch"), P(None, "ch"), P("ch"), P(), P()),
        out_specs=P(None, "ctx", "ch"),
        check_vma=False,
    )
```

```python
import jax
import jax.numpy as jnp
from jax import lax
from jax.experimental import pallas as pl
from jax.experimental.pallas import tpu as pltpu
from jax.sharding import PartitionSpec as P

MESH = pl.DeviceIdType.MESH
LANES = 128
TOK = 512
BLOCKS = TOK // LANES
RING = 32
CHUNKS = 4
HALF = 8
WIDTH = 2 * HALF
SPAN = 16
ROWS = RING * BLOCKS
LAGS = SPAN + 1
TAIL = SPAN // BLOCKS
STEPS = 8


def bordered(x, above, taps):
    place = lax.broadcasted_iota(jnp.int32, x.shape, 0)
    one = jnp.where(place == 0, above[1:2], pltpu.roll(x, 1, 0))
    two = jnp.where(place == 0, above[0:1], jnp.where(place == 1, above[1:2], pltpu.roll(x, 2, 0)))
    return taps[0:1] * x + taps[1:2] * one + taps[2:3] * two


def displacements():
    groups = [
        [(1, 0), (0, 1), (-1, 0), (0, -1)],
        [(1, 1), (-1, -1)],
        [(1, -1), (-1, 1)],
        [(2, 0), (0, 2)],
        [(2, 1), (1, 2), (2, -1), (-1, 2)],
        [(2, 2)],
    ]
    order = [(dx, dz, core) for core in (0, 1) for group in groups for dx, dz in group]
    return [(0, 0, 1)] + order


def fill_toeplitz(taps_ref, toep_ref, channel, slot):
    row = lax.broadcasted_iota(jnp.int32, (LANES, LANES), 0)
    col = lax.broadcasted_iota(jnp.int32, (LANES, LANES), 1)
    causal = col >= row
    older = jnp.zeros((LANES, LANES), jnp.bfloat16)
    for lag in range(LAGS):
        newer = jnp.zeros((LANES, LANES), jnp.bfloat16)
        if lag < SPAN:
            spread = jnp.broadcast_to(taps_ref[lag, pl.ds(channel, 1), :], (LANES, LANES))
            newer = pltpu.roll(spread, 0, 1, stride=1, stride_axis=0).astype(jnp.bfloat16)
        toep_ref[slot, lag * LANES : (lag + 1) * LANES] = jnp.where(causal, newer, older)
        older = newer


def convolve(wide_ref, toep_ref, mask_ref, total_ref, channel, slot):
    tiles = {
        u: wide_ref[pl.ds((SPAN + u) * WIDTH + channel, 16, stride=8 * WIDTH), :].astype(jnp.bfloat16)
        for u in range(-SPAN, 8)
    }
    columns = [
        jnp.concatenate([tiles[p - lag] for p in range(8)], axis=0) * mask_ref[lag]
        for lag in range(LAGS)
    ]
    left = jnp.concatenate(columns, axis=1)
    total = jnp.dot(left, toep_ref[slot], preferred_element_type=jnp.float32)
    for p in range(8):
        total_ref[pl.ds(p * WIDTH + channel, 16, stride=8 * WIDTH), :] = total[p * 16 : (p + 1) * 16]


def fill_mask(doc_ref, mask_ref, half):
    shape = (ROWS, LANES)
    index = lax.broadcasted_iota(jnp.int32, shape, 0)
    row = lax.rem(index, 16) * 8 + index // 16
    shard = row // BLOCKS + half * RING
    first = jnp.zeros(shape, jnp.int32)
    opened = jnp.int32(0)
    for spot in range(1, 2 * RING):
        opened = jnp.where(doc_ref[spot] != doc_ref[spot - 1], jnp.int32(spot), opened)
        first = jnp.where(shard == spot, opened, first)
    reach = row + half * ROWS - first * BLOCKS
    for lag in range(LAGS):
        mask_ref[lag] = jnp.where(reach >= lag, 1.0, 0.0).astype(jnp.bfloat16)


def fill_taps(columns, skip_ref, turned, taps_ref, direct_ref, ring):
    corner = lax.rem(ring, 4) * 32

    for part in range(2):
        @pl.loop(0, SPAN)
        def _(lag):
            at = pl.multiple_of(lag * LANES, LANES)
            turned[...] = columns[part, pl.ds(at, LANES), :].astype(jnp.float32).T
            for chunk in range(CHUNKS):
                to = chunk * WIDTH + part * HALF
                taps_ref[lag, to : to + HALF] = turned[pl.ds(pl.multiple_of(corner + chunk * HALF, 8), HALF)]

        line = skip_ref[pl.ds(part * 8 + ring // 4, 1), :]
        turned[...] = jnp.broadcast_to(line, (LANES, LANES)).T
        for chunk in range(CHUNKS):
            to = chunk * WIDTH + part * HALF
            direct_ref[to : to + HALF] = turned[pl.ds(pl.multiple_of(corner + chunk * HALF, 8), HALF)]


def exchange_kernel(
    doc_ref, live_ref, qkv_ref, short_ref, filter_ref, skip_ref, out_ref,
    raw, above, gated_ref, query_ref, columns, turned, taps_ref, direct_ref, mask_ref,
    got, edge, wide, total, ready, toep,
    load_sem, above_send, above_recv, column_sem,
    send_sem, recv_sem, edge_send, edge_recv, turn_send, turn_recv,
):
    place = lax.axis_index("ctx")
    group = lax.axis_index("ch")
    shards = lax.axis_size("ctx")
    half = place // RING
    ring = lax.rem(place, RING)
    x, z, core = ring // 8, lax.rem(ring // 2, 4), lax.rem(ring, 2)
    base = half * RING

    barrier = pltpu.get_barrier_semaphore()

    @pl.loop(1, RING)
    def _(k):
        peer = (base + lax.rem(ring + k, RING), group)
        pl.semaphore_signal(barrier, inc=1, device_id=peer, device_id_type=MESH)

    for other in range(2):
        @pl.when(jnp.logical_not((half == group) & (group == other)))
        def _():
            peer = (group * RING + ring, other)
            pl.semaphore_signal(barrier, inc=1, device_id=peer, device_id_type=MESH)

    @pl.when(half == 1)
    def _():
        pl.semaphore_signal(barrier, inc=1, device_id=(ring, group), device_id_type=MESH)

    @pl.when(place > 0)
    def _():
        pl.semaphore_signal(barrier, inc=1, device_id=(place - 1, group), device_id_type=MESH)

    def tile_of(step):
        near = step + 1
        return lax.rem(x + near // 2, 4) * 2 + lax.rem(z // 2 + near, 2)

    def load(step, slot, part):
        lane = pl.multiple_of(tile_of(step) * LANES + part * 8 * LANES, LANES)
        return pltpu.make_async_copy(
            qkv_ref.at[:, :, pl.ds(lane, LANES)], raw.at[slot, part], load_sem.at[slot, part]
        )

    def column(part):
        lane = pl.multiple_of((ring // 4) * LANES + part * 8 * LANES, LANES)
        return pltpu.make_async_copy(
            filter_ref.at[:, pl.ds(lane, LANES)], columns.at[part], column_sem.at[part]
        )

    above_copy = pltpu.make_async_remote_copy(
        src_ref=qkv_ref.at[:, pl.ds(TOK - 8, 8)],
        dst_ref=above,
        send_sem=above_send,
        recv_sem=above_recv,
        device_id=(lax.rem(place + 1, shards), group),
        device_id_type=MESH,
    )

    for part in range(2):
        load(0, 0, part).start()
    for part in range(2):
        column(part).start()

    @pl.when(place == 0)
    def _():
        above[...] = jnp.zeros_like(above)

    fill_mask(doc_ref, mask_ref, half)

    expected = RING - 1 + jnp.where(half == group, 1, 2) + jnp.where(half == 0, 1, 0)
    expected = expected + jnp.where(place < shards - 1, 1, 0)
    pl.semaphore_wait(barrier, expected)

    @pl.when(place < shards - 1)
    def _():
        above_copy.start()

    sources = (gated_ref, query_ref)

    def send(chunk, kind):
        for dx, dz, dc in displacements():
            to = (lax.rem(x + dx + 4, 4) * 4 + lax.rem(z + dz + 4, 4)) * 2 + lax.rem(core + dc, 2)
            pltpu.make_async_remote_copy(
                src_ref=sources[kind].at[chunk, to],
                dst_ref=got.at[chunk, kind, ring],
                send_sem=send_sem.at[chunk, kind],
                recv_sem=recv_sem.at[chunk, kind],
                device_id=(base + to, group),
                device_id_type=MESH,
            ).start()
        pltpu.make_async_copy(
            sources[kind].at[chunk, ring], got.at[chunk, kind, ring], recv_sem.at[chunk, kind]
        ).start()

    def send_tile(tile, chunk, kind):
        for member in range(4):
            to = tile * 4 + member

            @pl.when(to == ring)
            def _():
                pltpu.make_async_copy(
                    sources[kind].at[chunk, to], got.at[chunk, kind, to], recv_sem.at[chunk, kind]
                ).start()

            @pl.when(to != ring)
            def _():
                pltpu.make_async_remote_copy(
                    src_ref=sources[kind].at[chunk, to],
                    dst_ref=got.at[chunk, kind, ring],
                    send_sem=send_sem.at[chunk, kind],
                    recv_sem=recv_sem.at[chunk, kind],
                    device_id=(base + to, group),
                    device_id_type=MESH,
                ).start()

    def arrived(chunk, kind):
        pltpu.make_async_copy(
            sources[kind].at[chunk], got.at[chunk, kind], recv_sem.at[chunk, kind]
        ).wait()

    def edge_copy(chunk):
        return pltpu.make_async_remote_copy(
            src_ref=got.at[chunk, 0, pl.ds(RING - TAIL, TAIL)],
            dst_ref=edge.at[chunk],
            send_sem=edge_send.at[chunk],
            recv_sem=edge_recv.at[chunk],
            device_id=(RING + ring, group),
            device_id_type=MESH,
        )

    def turn_copy(chunk, part):
        return pltpu.make_async_remote_copy(
            src_ref=ready.at[chunk, part],
            dst_ref=out_ref.at[group, pl.ds(chunk * HALF, HALF)],
            send_sem=turn_send.at[chunk, part],
            recv_sem=turn_recv.at[0],
            device_id=(part * RING + ring, half),
            device_id_type=MESH,
        )

    doc_here = doc_ref[place]
    joined = (place > 0) & (doc_ref[jnp.maximum(place - 1, 0)] == doc_here)
    linked = jnp.where(joined, 1.0, 0.0).astype(jnp.float32)
    closing = (place == shards - 1) | (doc_ref[jnp.minimum(place + 1, shards - 1)] != doc_here)
    limit = jnp.where(closing, live_ref[place], TOK)

    @pl.when(place > 0)
    def _():
        above_copy.wait_recv()

    @pl.loop(0, STEPS)
    def _(step):
        slot = lax.rem(step, 2)
        tile = tile_of(step)
        keep = jnp.where(
            lax.broadcasted_iota(jnp.int32, (TOK, LANES), 0) < limit, 1.0, 0.0
        ).astype(jnp.float32)

        @pl.when(step + 1 < STEPS)
        def _():
            for part in range(2):
                load(step + 1, 1 - slot, part).start()

        gates = []
        for part in range(2):
            load(step, slot, part).wait()
            lane = pl.multiple_of(tile * LANES + part * 8 * LANES, LANES)
            parts = [
                bordered(
                    raw[slot, part, a].astype(jnp.float32),
                    above[a, :, pl.ds(lane, LANES)].astype(jnp.float32)[6:8] * linked,
                    short_ref[a, :, pl.ds(lane, LANES)],
                )
                for a in range(3)
            ]
            query = parts[0].astype(jnp.bfloat16).astype(jnp.float32) * keep
            gates.append((parts[1] * parts[2] * keep, query))
        for which in range(2):
            for block in range(BLOCKS):
                rows = slice(block * LANES, (block + 1) * LANES)
                first = gates[0][which][rows].T
                second = gates[1][which][rows].T
                for peer in range(4):
                    for chunk in range(CHUNKS):
                        at = peer * 32 + chunk * HALF
                        both = jnp.concatenate(
                            [first[at : at + HALF], second[at : at + HALF]], axis=0
                        )
                        sources[which][chunk, tile * 4 + peer, block] = both.astype(jnp.bfloat16)
        send_tile(tile, 0, 0)
        send_tile(tile, 1, 0)

    for chunk, kind in ((0, 1), (2, 0), (1, 1), (3, 0), (2, 1), (3, 1)):
        send(chunk, kind)

    for part in range(2):
        column(part).wait()
    fill_taps(columns, skip_ref, turned, taps_ref, direct_ref, ring)

    @pl.loop(0, CHUNKS)
    def _(chunk):
        arrived(chunk, 0)

        @pl.when(half == 0)
        def _():
            edge_copy(chunk).start()
            wide[pl.ds(0, SPAN * WIDTH)] = jnp.zeros((SPAN * WIDTH, LANES), jnp.float32)

        @pl.loop(0, RING)
        def _(shard):
            at = pl.multiple_of((SPAN + shard * BLOCKS) * WIDTH, 8)
            wide[pl.ds(at, BLOCKS * WIDTH)] = (
                got[chunk, 0, shard].reshape(BLOCKS * WIDTH, LANES).astype(jnp.float32)
            )

        @pl.when(half == 1)
        def _():
            edge_copy(chunk).wait_recv()
            for shard in range(TAIL):
                wide[shard * BLOCKS * WIDTH : (shard + 1) * BLOCKS * WIDTH] = (
                    edge[chunk, shard].reshape(BLOCKS * WIDTH, LANES).astype(jnp.float32)
                )

        @pl.loop(0, WIDTH // 4)
        def _(four):
            for i in range(4):
                fill_toeplitz(taps_ref, toep, chunk * WIDTH + four * 4 + i, i)
            for i in range(4):
                convolve(wide, toep, mask_ref, total, four * 4 + i, i)

        arrived(chunk, 1)
        direct = direct_ref[pl.ds(pl.multiple_of(chunk * WIDTH, WIDTH), WIDTH)]

        @pl.loop(0, RING)
        def _(shard):
            for block in range(BLOCKS):
                row = shard * BLOCKS + block
                at = pl.multiple_of(row * WIDTH, WIDTH)
                gated = got[chunk, 0, shard, block].astype(jnp.float32)
                query = got[chunk, 1, shard, block].astype(jnp.float32)
                value = (query * (total[pl.ds(at, WIDTH)] + direct * gated)).astype(jnp.bfloat16)
                to = pl.multiple_of(row * LANES, LANES)
                ready[chunk, 0, :, pl.ds(to, LANES)] = value[:HALF]
                ready[chunk, 1, :, pl.ds(to, LANES)] = value[HALF:]

        for part in range(2):
            stays = (half == group) & (half == part)

            @pl.when(stays)
            def _():
                pltpu.make_async_copy(
                    ready.at[chunk, part],
                    out_ref.at[group, pl.ds(chunk * HALF, HALF)],
                    turn_recv.at[0],
                ).start()

            @pl.when(jnp.logical_not(stays))
            def _():
                turn_copy(chunk, part).start()

    @pl.loop(0, CHUNKS)
    def _(chunk):
        for kind in range(2):
            pltpu.make_async_remote_copy(
                src_ref=sources[kind].at[chunk, pl.ds(0, RING - 1)],
                dst_ref=got.at[chunk, kind, pl.ds(0, RING - 1)],
                send_sem=send_sem.at[chunk, kind],
                recv_sem=recv_sem.at[chunk, kind],
                device_id=(place, group),
                device_id_type=MESH,
            ).wait_send()
        for part in range(2):
            @pl.when(jnp.logical_not((half == group) & (half == part)))
            def _():
                turn_copy(chunk, part).wait_send()

        @pl.when(half == 0)
        def _():
            edge_copy(chunk).wait_send()

    @pl.when(place < shards - 1)
    def _():
        above_copy.wait_send()

    pltpu.make_async_copy(out_ref, out_ref, turn_recv.at[0]).wait()


def local(qkv, short_filter, long_filter, skip, shard_doc, live):
    vmem = pl.BlockSpec(memory_space=pltpu.VMEM)
    smem = pl.BlockSpec(memory_space=pltpu.SMEM)
    hbm = pl.BlockSpec(memory_space=pl.ANY)
    dma = pltpu.SemaphoreType.DMA
    tokens = ROWS * LANES
    parcel = (CHUNKS, RING, BLOCKS, WIDTH, LANES)
    return pl.pallas_call(
        exchange_kernel,
        out_shape=jax.ShapeDtypeStruct((2, CHUNKS * HALF, tokens), jnp.bfloat16),
        in_specs=[smem, smem, hbm, vmem, hbm, vmem],
        out_specs=hbm,
        scratch_shapes=[
            pltpu.VMEM((2, 2, 3, TOK, LANES), jnp.bfloat16),
            pltpu.VMEM((3, 8, qkv.shape[2]), jnp.bfloat16),
            pltpu.VMEM(parcel, jnp.bfloat16),
            pltpu.VMEM(parcel, jnp.bfloat16),
            pltpu.VMEM((2, SPAN * LANES, LANES), jnp.bfloat16),
            pltpu.VMEM((LANES, LANES), jnp.float32),
            pltpu.VMEM((SPAN, CHUNKS * WIDTH, LANES), jnp.float32),
            pltpu.VMEM((CHUNKS * WIDTH, LANES), jnp.float32),
            pltpu.VMEM((LAGS, ROWS, LANES), jnp.bfloat16),
            pltpu.VMEM((CHUNKS, 2, RING, BLOCKS, WIDTH, LANES), jnp.bfloat16),
            pltpu.VMEM((CHUNKS, TAIL, BLOCKS, WIDTH, LANES), jnp.bfloat16),
            pltpu.VMEM(((SPAN + ROWS) * WIDTH, LANES), jnp.float32),
            pltpu.VMEM((ROWS * WIDTH, LANES), jnp.float32),
            pltpu.VMEM((CHUNKS, 2, HALF, tokens), jnp.bfloat16),
            pltpu.VMEM((4, LAGS * LANES, LANES), jnp.bfloat16),
            dma((2, 2)),
            dma,
            dma,
            dma((2,)),
            dma((CHUNKS, 2)),
            dma((CHUNKS, 2)),
            dma((CHUNKS,)),
            dma((CHUNKS,)),
            dma((CHUNKS, 2)),
            dma((1,)),
        ],
        compiler_params=pltpu.CompilerParams(
            collective_id=0, has_side_effects=True, vmem_limit_bytes=56 * 2**20
        ),
    )(shard_doc, live, qkv, short_filter, long_filter, skip.reshape(-1, LANES))


def solution(mesh):
    return jax.shard_map(
        local,
        mesh=mesh,
        in_specs=(P(None, "ctx", "ch"), P(None, None, "ch"), P(None, "ch"), P("ch"), P(), P()),
        out_specs=P(None, "ctx", "ch"),
        check_vma=False,
    )
```

```python
import jax
import jax.numpy as jnp
from jax import lax
from jax.experimental import pallas as pl
from jax.experimental.pallas import tpu as pltpu
from jax.sharding import PartitionSpec as P

MESH = pl.DeviceIdType.MESH
LANES = 128
TOK = 512
BLOCKS = TOK // LANES
RING = 32
CHUNKS = 8
HALF = 4
WIDTH = 2 * HALF
SPAN = 16
ROWS = RING * BLOCKS
LAGS = SPAN + 1
TAIL = SPAN // BLOCKS
STEPS = 8
PIECES = 4
LEG = 1
PIECE = ROWS // PIECES


def bordered(x, above, taps):
    place = lax.broadcasted_iota(jnp.int32, x.shape, 0)
    one = jnp.where(place == 0, above[1:2], pltpu.roll(x, 1, 0))
    two = jnp.where(place == 0, above[0:1], jnp.where(place == 1, above[1:2], pltpu.roll(x, 2, 0)))
    return taps[0:1] * x + taps[1:2] * one + taps[2:3] * two


def displacements():
    groups = [
        [(1, 1), (-1, -1), (1, -1), (-1, 1)],
        [(2, 1), (1, 2), (2, -1), (-1, 2)],
        [(1, 0), (0, 1), (-1, 0), (0, -1)],
        [(2, 2), (2, 0), (0, 2)],
    ]
    order = [(dx, dz, core) for core in (0, 1) for group in groups for dx, dz in group]
    return order + [(0, 0, 1)]


def fill_toeplitz(taps_ref, toep_ref, channel, slot):
    row = lax.broadcasted_iota(jnp.int32, (LANES, LANES), 0)
    col = lax.broadcasted_iota(jnp.int32, (LANES, LANES), 1)
    causal = col >= row
    older = jnp.zeros((LANES, LANES), jnp.bfloat16)
    for lag in range(LAGS):
        newer = jnp.zeros((LANES, LANES), jnp.bfloat16)
        if lag < SPAN:
            spread = jnp.broadcast_to(taps_ref[lag, pl.ds(channel, 1), :], (LANES, LANES))
            newer = pltpu.roll(spread, 0, 1, stride=1, stride_axis=0).astype(jnp.bfloat16)
        toep_ref[slot, lag * LANES : (lag + 1) * LANES] = jnp.where(causal, newer, older)
        older = newer


def convolve(wide_ref, toep_ref, mask_ref, total_ref, channel, slot):
    tiles = {
        u: wide_ref[pl.ds((SPAN + u) * WIDTH + channel, 16, stride=8 * WIDTH), :].astype(jnp.bfloat16)
        for u in range(-SPAN, 8)
    }
    columns = [
        jnp.concatenate([tiles[p - lag] for p in range(8)], axis=0) * mask_ref[lag]
        for lag in range(LAGS)
    ]
    left = jnp.concatenate(columns, axis=1)
    total = jnp.dot(left, toep_ref[slot], preferred_element_type=jnp.float32)
    for p in range(8):
        total_ref[pl.ds(p * WIDTH + channel, 16, stride=8 * WIDTH), :] = total[p * 16 : (p + 1) * 16]


def fill_mask(doc_ref, mask_ref, half):
    shape = (ROWS, LANES)
    index = lax.broadcasted_iota(jnp.int32, shape, 0)
    row = lax.rem(index, 16) * 8 + index // 16
    shard = row // BLOCKS + half * RING
    first = jnp.zeros(shape, jnp.int32)
    opened = jnp.int32(0)
    for spot in range(1, 2 * RING):
        opened = jnp.where(doc_ref[spot] != doc_ref[spot - 1], jnp.int32(spot), opened)
        first = jnp.where(shard == spot, opened, first)
    reach = row + half * ROWS - first * BLOCKS
    for lag in range(LAGS):
        mask_ref[lag] = jnp.where(reach >= lag, 1.0, 0.0).astype(jnp.bfloat16)


def fill_taps(columns, skip_ref, turned, taps_ref, direct_ref, ring):
    corner = lax.rem(ring, 4) * 32

    for part in range(2):
        @pl.loop(0, SPAN)
        def _(lag):
            at = pl.multiple_of(lag * LANES, LANES)
            turned[...] = columns[part, pl.ds(at, LANES), :].astype(jnp.float32).T
            for chunk in range(CHUNKS):
                to = chunk * WIDTH + part * HALF
                taps_ref[lag, to : to + HALF] = turned[pl.ds(pl.multiple_of(corner + chunk // 2 * 8, 8), 8)][chunk % 2 * HALF : chunk % 2 * HALF + HALF]

        line = skip_ref[pl.ds(part * 8 + ring // 4, 1), :]
        turned[...] = jnp.broadcast_to(line, (LANES, LANES)).T
        for chunk in range(CHUNKS):
            to = chunk * WIDTH + part * HALF
            direct_ref[to : to + HALF] = turned[pl.ds(pl.multiple_of(corner + chunk // 2 * 8, 8), 8)][chunk % 2 * HALF : chunk % 2 * HALF + HALF]


def exchange_kernel(
    doc_ref, live_ref, qkv_ref, short_ref, filter_ref, skip_ref, out_ref,
    raw, above, gated_ref, query_ref, columns, turned, taps_ref, direct_ref, mask_ref,
    got, edge, wide, total, ready, relay, toep,
    load_sem, above_send, above_recv, column_sem,
    send_sem, recv_sem, edge_send, edge_recv, turn_send, turn_recv, relay_send, relay_recv,
):
    place = lax.axis_index("ctx")
    group = lax.axis_index("ch")
    shards = lax.axis_size("ctx")
    half = place // RING
    ring = lax.rem(place, RING)
    x, z, core = ring // 8, lax.rem(ring // 2, 4), lax.rem(ring, 2)
    base = half * RING

    barrier = pltpu.get_barrier_semaphore()

    @pl.loop(1, RING)
    def _(k):
        peer = (base + lax.rem(ring + k, RING), group)
        pl.semaphore_signal(barrier, inc=1, device_id=peer, device_id_type=MESH)

    for part in range(2):
        peer = (part * RING + ring, 1 - group)
        pl.semaphore_signal(barrier, inc=1, device_id=peer, device_id_type=MESH)

    @pl.when(half == 1)
    def _():
        pl.semaphore_signal(barrier, inc=1, device_id=(ring, group), device_id_type=MESH)

    @pl.when(place > 0)
    def _():
        pl.semaphore_signal(barrier, inc=1, device_id=(place - 1, group), device_id_type=MESH)

    def tile_of(step):
        near = step + 1
        return lax.rem(x + near // 2, 4) * 2 + lax.rem(z // 2 + near, 2)

    def load(step, slot, part):
        lane = pl.multiple_of(tile_of(step) * LANES + part * 8 * LANES, LANES)
        return pltpu.make_async_copy(
            qkv_ref.at[:, :, pl.ds(lane, LANES)], raw.at[slot, part], load_sem.at[slot, part]
        )

    def column(part):
        lane = pl.multiple_of((ring // 4) * LANES + part * 8 * LANES, LANES)
        return pltpu.make_async_copy(
            filter_ref.at[:, pl.ds(lane, LANES)], columns.at[part], column_sem.at[part]
        )

    above_copy = pltpu.make_async_remote_copy(
        src_ref=qkv_ref.at[:, pl.ds(TOK - 8, 8)],
        dst_ref=above,
        send_sem=above_send,
        recv_sem=above_recv,
        device_id=(lax.rem(place + 1, shards), group),
        device_id_type=MESH,
    )

    for part in range(2):
        load(0, 0, part).start()
    for part in range(2):
        column(part).start()

    @pl.when(place == 0)
    def _():
        above[...] = jnp.zeros_like(above)

    fill_mask(doc_ref, mask_ref, half)

    expected = RING + 1 + jnp.where(half == 0, 1, 0)
    expected = expected + jnp.where(place < shards - 1, 1, 0)
    pl.semaphore_wait(barrier, expected)

    @pl.when(place < shards - 1)
    def _():
        above_copy.start()

    sources = (gated_ref, query_ref)

    def send(chunk, kind):
        for dx, dz, dc in displacements():
            to = (lax.rem(x + dx + 4, 4) * 4 + lax.rem(z + dz + 4, 4)) * 2 + lax.rem(core + dc, 2)
            pltpu.make_async_remote_copy(
                src_ref=sources[kind].at[chunk, to],
                dst_ref=got.at[chunk, kind, ring],
                send_sem=send_sem.at[chunk, kind],
                recv_sem=recv_sem.at[chunk, kind],
                device_id=(base + to, group),
                device_id_type=MESH,
            ).start()
        pltpu.make_async_copy(
            sources[kind].at[chunk, ring], got.at[chunk, kind, ring], recv_sem.at[chunk, kind]
        ).start()

    def send_tile(tile, chunk, kind):
        for member in range(4):
            to = tile * 4 + member

            @pl.when(to == ring)
            def _():
                pltpu.make_async_copy(
                    sources[kind].at[chunk, to], got.at[chunk, kind, to], recv_sem.at[chunk, kind]
                ).start()

            @pl.when(to != ring)
            def _():
                pltpu.make_async_remote_copy(
                    src_ref=sources[kind].at[chunk, to],
                    dst_ref=got.at[chunk, kind, ring],
                    send_sem=send_sem.at[chunk, kind],
                    recv_sem=recv_sem.at[chunk, kind],
                    device_id=(base + to, group),
                    device_id_type=MESH,
                ).start()

    def arrived(chunk, kind):
        pltpu.make_async_copy(
            sources[kind].at[chunk], got.at[chunk, kind], recv_sem.at[chunk, kind]
        ).wait()

    def edge_copy(chunk):
        return pltpu.make_async_remote_copy(
            src_ref=got.at[chunk, 0, pl.ds(RING - TAIL, TAIL)],
            dst_ref=edge.at[chunk],
            send_sem=edge_send.at[chunk],
            recv_sem=edge_recv.at[chunk],
            device_id=(RING + ring, group),
            device_id_type=MESH,
        )

    corner = half == group

    def span_of(piece, count=1):
        return pl.ds(piece * PIECE, PIECE * count)

    def turn(chunk, part, piece):
        span = span_of(piece)
        source = ready.at[chunk, part, span]

        @pl.when(jnp.logical_not(corner))
        def _():
            pltpu.make_async_remote_copy(
                src_ref=source,
                dst_ref=out_ref.at[group, chunk, span],
                send_sem=turn_send.at[chunk, part],
                recv_sem=turn_recv.at[0],
                device_id=(part * RING + ring, 1 - group),
                device_id_type=MESH,
            ).start()

        @pl.when(corner & (half == part))
        def _():
            pltpu.make_async_copy(
                source, out_ref.at[group, chunk, span], turn_recv.at[0]
            ).start()

        @pl.when(corner & (half != part))
        def _():
            pltpu.make_async_remote_copy(
                src_ref=source,
                dst_ref=relay.at[chunk, span],
                send_sem=turn_send.at[chunk, part],
                recv_sem=relay_recv.at[chunk, piece // LEG],
                device_id=(part * RING + ring, 1 - group),
                device_id_type=MESH,
            ).start()

    def forward(chunk):
        @pl.when(corner)
        def _():
            for leg in range(PIECES // LEG):
                span = span_of(leg * LEG, LEG)
                copy = pltpu.make_async_remote_copy(
                    src_ref=relay.at[chunk, span],
                    dst_ref=out_ref.at[1 - group, chunk, span],
                    send_sem=relay_send.at[chunk],
                    recv_sem=turn_recv.at[0],
                    device_id=(half * RING + ring, 1 - group),
                    device_id_type=MESH,
                )
                pltpu.make_async_copy(
                    ready.at[chunk, 0, span], relay.at[chunk, span], relay_recv.at[chunk, leg]
                ).wait()
                copy.start()

    doc_here = doc_ref[place]
    joined = (place > 0) & (doc_ref[jnp.maximum(place - 1, 0)] == doc_here)
    linked = jnp.where(joined, 1.0, 0.0).astype(jnp.float32)
    closing = (place == shards - 1) | (doc_ref[jnp.minimum(place + 1, shards - 1)] != doc_here)
    limit = jnp.where(closing, live_ref[place], TOK)

    @pl.when(place > 0)
    def _():
        above_copy.wait_recv()

    @pl.loop(0, STEPS)
    def _(step):
        slot = lax.rem(step, 2)
        tile = tile_of(step)
        keep = jnp.where(
            lax.broadcasted_iota(jnp.int32, (TOK, LANES), 0) < limit, 1.0, 0.0
        ).astype(jnp.float32)

        @pl.when(step + 1 < STEPS)
        def _():
            for part in range(2):
                load(step + 1, 1 - slot, part).start()

        gates = []
        for part in range(2):
            load(step, slot, part).wait()
            lane = pl.multiple_of(tile * LANES + part * 8 * LANES, LANES)
            parts = [
                bordered(
                    raw[slot, part, a].astype(jnp.float32),
                    above[a, :, pl.ds(lane, LANES)].astype(jnp.float32)[6:8] * linked,
                    short_ref[a, :, pl.ds(lane, LANES)],
                )
                for a in range(3)
            ]
            query = parts[0].astype(jnp.bfloat16).astype(jnp.float32) * keep
            gates.append((parts[1] * parts[2] * keep, query))
        for which in range(2):
            for block in range(BLOCKS):
                rows = slice(block * LANES, (block + 1) * LANES)
                first = gates[0][which][rows].T
                second = gates[1][which][rows].T
                for peer in range(4):
                    for chunk in range(CHUNKS):
                        at = peer * 32 + chunk * HALF
                        both = jnp.concatenate(
                            [first[at : at + HALF], second[at : at + HALF]], axis=0
                        )
                        sources[which][chunk, tile * 4 + peer, block] = both.astype(jnp.bfloat16)
        send_tile(tile, 0, 0)
        send_tile(tile, 1, 0)

    send(0, 1)
    send(1, 1)

    @pl.loop(2, CHUNKS)
    def _(chunk):
        send(chunk, 0)
        send(chunk, 1)

    for part in range(2):
        column(part).wait()
    fill_taps(columns, skip_ref, turned, taps_ref, direct_ref, ring)

    def long_conv(chunk):
        arrived(chunk, 0)

        @pl.when(half == 0)
        def _():
            edge_copy(chunk).start()
            wide[pl.ds(0, SPAN * WIDTH)] = jnp.zeros((SPAN * WIDTH, LANES), jnp.float32)

        @pl.loop(0, RING)
        def _(shard):
            at = pl.multiple_of((SPAN + shard * BLOCKS) * WIDTH, 8)
            wide[pl.ds(at, BLOCKS * WIDTH)] = (
                got[chunk, 0, shard].reshape(BLOCKS * WIDTH, LANES).astype(jnp.float32)
            )

        @pl.when(half == 1)
        def _():
            edge_copy(chunk).wait_recv()
            for shard in range(TAIL):
                wide[shard * BLOCKS * WIDTH : (shard + 1) * BLOCKS * WIDTH] = (
                    edge[chunk, shard].reshape(BLOCKS * WIDTH, LANES).astype(jnp.float32)
                )

        @pl.loop(0, WIDTH // 4)
        def _(four):
            for i in range(4):
                fill_toeplitz(taps_ref, toep, chunk * WIDTH + four * 4 + i, i)
            for i in range(4):
                convolve(wide, toep, mask_ref, total.at[lax.rem(chunk, 2)], four * 4 + i, i)

    def product(chunk):
        arrived(chunk, 1)
        direct = direct_ref[pl.ds(pl.multiple_of(chunk * WIDTH, WIDTH), WIDTH)]
        for piece in range(PIECES):
            @pl.loop(0, RING // PIECES)
            def _(offset):
                shard = piece * (RING // PIECES) + offset
                for block in range(BLOCKS):
                    row = shard * BLOCKS + block
                    at = pl.multiple_of(row * WIDTH, WIDTH)
                    gated = got[chunk, 0, shard, block].astype(jnp.float32)
                    query = got[chunk, 1, shard, block].astype(jnp.float32)
                    value = query * (total[lax.rem(chunk, 2), pl.ds(at, WIDTH)] + direct * gated)
                    ready[chunk, 0, row] = value[:HALF].astype(jnp.bfloat16)
                    ready[chunk, 1, row] = value[HALF:].astype(jnp.bfloat16)

            for part in range(2):
                turn(chunk, part, piece)

    @pl.loop(0, CHUNKS)
    def _(chunk):
        long_conv(chunk)
        product(chunk)

        @pl.when(chunk > 0)
        def _():
            forward(chunk - 1)

    forward(CHUNKS - 1)

    @pl.loop(0, CHUNKS)
    def _(chunk):
        for kind in range(2):
            pltpu.make_async_remote_copy(
                src_ref=sources[kind].at[chunk, pl.ds(0, RING - 1)],
                dst_ref=got.at[chunk, kind, pl.ds(0, RING - 1)],
                send_sem=send_sem.at[chunk, kind],
                recv_sem=recv_sem.at[chunk, kind],
                device_id=(place, group),
                device_id_type=MESH,
            ).wait_send()
        def drained(source, sem):
            pltpu.make_async_remote_copy(
                src_ref=source,
                dst_ref=source,
                send_sem=sem,
                recv_sem=turn_recv.at[0],
                device_id=(place, group),
                device_id_type=MESH,
            ).wait_send()

        for part in range(2):
            @pl.when(jnp.logical_not(corner & (half == part)))
            def _():
                drained(ready.at[chunk, part], turn_send.at[chunk, part])

        @pl.when(corner)
        def _():
            drained(relay.at[chunk], relay_send.at[chunk])

        @pl.when(half == 0)
        def _():
            edge_copy(chunk).wait_send()

    @pl.when(place < shards - 1)
    def _():
        above_copy.wait_send()

    pltpu.make_async_copy(out_ref, out_ref, turn_recv.at[0]).wait()


def local(qkv, short_filter, long_filter, skip, shard_doc, live):
    vmem = pl.BlockSpec(memory_space=pltpu.VMEM)
    smem = pl.BlockSpec(memory_space=pltpu.SMEM)
    hbm = pl.BlockSpec(memory_space=pl.ANY)
    dma = pltpu.SemaphoreType.DMA
    parcel = (CHUNKS, RING, BLOCKS, WIDTH, LANES)
    moved = pl.pallas_call(
        exchange_kernel,
        out_shape=jax.ShapeDtypeStruct((2, CHUNKS, ROWS, HALF, LANES), jnp.bfloat16),
        in_specs=[smem, smem, hbm, vmem, hbm, vmem],
        out_specs=hbm,
        scratch_shapes=[
            pltpu.VMEM((2, 2, 3, TOK, LANES), jnp.bfloat16),
            pltpu.VMEM((3, 8, qkv.shape[2]), jnp.bfloat16),
            pltpu.VMEM(parcel, jnp.bfloat16),
            pltpu.VMEM(parcel, jnp.bfloat16),
            pltpu.VMEM((2, SPAN * LANES, LANES), jnp.bfloat16),
            pltpu.VMEM((LANES, LANES), jnp.float32),
            pltpu.VMEM((SPAN, CHUNKS * WIDTH, LANES), jnp.float32),
            pltpu.VMEM((CHUNKS * WIDTH, LANES), jnp.float32),
            pltpu.VMEM((LAGS, ROWS, LANES), jnp.bfloat16),
            pltpu.VMEM((CHUNKS, 2, RING, BLOCKS, WIDTH, LANES), jnp.bfloat16),
            pltpu.VMEM((CHUNKS, TAIL, BLOCKS, WIDTH, LANES), jnp.bfloat16),
            pltpu.VMEM(((SPAN + ROWS) * WIDTH, LANES), jnp.float32),
            pltpu.VMEM((2, ROWS * WIDTH, LANES), jnp.float32),
            pltpu.VMEM((CHUNKS, 2, ROWS, HALF, LANES), jnp.bfloat16),
            pltpu.VMEM((CHUNKS, ROWS, HALF, LANES), jnp.bfloat16),
            pltpu.VMEM((4, LAGS * LANES, LANES), jnp.bfloat16),
            dma((2, 2)),
            dma,
            dma,
            dma((2,)),
            dma((CHUNKS, 2)),
            dma((CHUNKS, 2)),
            dma((CHUNKS,)),
            dma((CHUNKS,)),
            dma((CHUNKS, 2)),
            dma((1,)),
            dma((CHUNKS,)),
            dma((CHUNKS, PIECES // LEG)),
        ],
        compiler_params=pltpu.CompilerParams(
            collective_id=0, has_side_effects=True, vmem_limit_bytes=60 * 2**20
        ),
    )(shard_doc, live, qkv, short_filter, long_filter, skip.reshape(-1, LANES))
    return moved.transpose(0, 1, 3, 2, 4).reshape(2, CHUNKS * HALF, ROWS * LANES)


def solution(mesh):
    return jax.shard_map(
        local,
        mesh=mesh,
        in_specs=(P(None, "ctx", "ch"), P(None, None, "ch"), P(None, "ch"), P("ch"), P(), P()),
        out_specs=P(None, "ctx", "ch"),
        check_vma=False,
    )
```

```python
import jax
import jax.numpy as jnp
from jax import lax
from jax.experimental import pallas as pl
from jax.experimental.pallas import tpu as pltpu
from jax.sharding import PartitionSpec as P

MESH = pl.DeviceIdType.MESH
LANES = 128
TOK = 512
BLOCKS = TOK // LANES
RING = 32
CHUNKS = 8
HALF = 4
WIDTH = 2 * HALF
SPAN = 16
ROWS = RING * BLOCKS
LAGS = SPAN + 1
TAIL = SPAN // BLOCKS
STEPS = 8
AHEAD = 4
PIECES = 4
LEG = 1
PIECE = ROWS // PIECES


def bordered(x, above, taps):
    place = lax.broadcasted_iota(jnp.int32, x.shape, 0)
    one = jnp.where(place == 0, above[1:2], pltpu.roll(x, 1, 0))
    two = jnp.where(place == 0, above[0:1], jnp.where(place == 1, above[1:2], pltpu.roll(x, 2, 0)))
    return taps[0:1] * x + taps[1:2] * one + taps[2:3] * two


def displacements():
    groups = [
        [(1, 1), (-1, -1), (1, -1), (-1, 1)],
        [(2, 1), (1, 2), (2, -1), (-1, 2)],
        [(1, 0), (0, 1), (-1, 0), (0, -1)],
        [(2, 2), (2, 0), (0, 2)],
    ]
    order = [(dx, dz, core) for core in (0, 1) for group in groups for dx, dz in group]
    return order + [(0, 0, 1)]


def fill_toeplitz(taps_ref, toep_ref, channel, slot):
    row = lax.broadcasted_iota(jnp.int32, (LANES, LANES), 0)
    col = lax.broadcasted_iota(jnp.int32, (LANES, LANES), 1)
    causal = col >= row
    older = jnp.zeros((LANES, LANES), jnp.bfloat16)
    for lag in range(LAGS):
        newer = jnp.zeros((LANES, LANES), jnp.bfloat16)
        if lag < SPAN:
            spread = jnp.broadcast_to(taps_ref[lag, pl.ds(channel, 1), :], (LANES, LANES))
            newer = pltpu.roll(spread, 0, 1, stride=1, stride_axis=0).astype(jnp.bfloat16)
        toep_ref[slot, lag * LANES : (lag + 1) * LANES] = jnp.where(causal, newer, older)
        older = newer


def convolve(wide_ref, toep_ref, mask_ref, total_ref, channel, slot):
    tiles = {
        u: wide_ref[pl.ds((SPAN + u) * WIDTH + channel, 16, stride=8 * WIDTH), :].astype(jnp.bfloat16)
        for u in range(-SPAN, 8)
    }
    columns = [
        jnp.concatenate([tiles[p - lag] for p in range(8)], axis=0) * mask_ref[lag]
        for lag in range(LAGS)
    ]
    left = jnp.concatenate(columns, axis=1)
    total = jnp.dot(left, toep_ref[slot], preferred_element_type=jnp.float32)
    for p in range(8):
        total_ref[pl.ds(p * WIDTH + channel, 16, stride=8 * WIDTH), :] = total[p * 16 : (p + 1) * 16]


def fill_mask(doc_ref, mask_ref, half):
    shape = (ROWS, LANES)
    index = lax.broadcasted_iota(jnp.int32, shape, 0)
    row = lax.rem(index, 16) * 8 + index // 16
    shard = row // BLOCKS + half * RING
    first = jnp.zeros(shape, jnp.int32)
    opened = jnp.int32(0)
    for spot in range(1, 2 * RING):
        opened = jnp.where(doc_ref[spot] != doc_ref[spot - 1], jnp.int32(spot), opened)
        first = jnp.where(shard == spot, opened, first)
    reach = row + half * ROWS - first * BLOCKS
    for lag in range(LAGS):
        mask_ref[lag] = jnp.where(reach >= lag, 1.0, 0.0).astype(jnp.bfloat16)


def fill_taps(columns, skip_ref, turned, taps_ref, direct_ref, ring):
    corner = lax.rem(ring, 4) * 32

    for part in range(2):
        @pl.loop(0, SPAN)
        def _(lag):
            at = pl.multiple_of(lag * LANES, LANES)
            turned[...] = columns[part, pl.ds(at, LANES), :].astype(jnp.float32).T
            for chunk in range(CHUNKS):
                to = chunk * WIDTH + part * HALF
                taps_ref[lag, to : to + HALF] = turned[pl.ds(pl.multiple_of(corner + chunk // 2 * 8, 8), 8)][chunk % 2 * HALF : chunk % 2 * HALF + HALF]

        line = skip_ref[pl.ds(part * 8 + ring // 4, 1), :]
        turned[...] = jnp.broadcast_to(line, (LANES, LANES)).T
        for chunk in range(CHUNKS):
            to = chunk * WIDTH + part * HALF
            direct_ref[to : to + HALF] = turned[pl.ds(pl.multiple_of(corner + chunk // 2 * 8, 8), 8)][chunk % 2 * HALF : chunk % 2 * HALF + HALF]


def exchange_kernel(
    doc_ref, live_ref, qkv_ref, short_ref, filter_ref, skip_ref, out_ref,
    raw, above, gated_ref, query_ref, columns, turned, taps_ref, direct_ref, mask_ref,
    got, edge, wide, total, ready, relay, toep,
    load_sem, above_send, above_recv, column_sem,
    send_sem, recv_sem, edge_send, edge_recv, turn_send, turn_recv, relay_send, relay_recv,
):
    place = lax.axis_index("ctx")
    group = lax.axis_index("ch")
    shards = lax.axis_size("ctx")
    half = place // RING
    ring = lax.rem(place, RING)
    x, z, core = ring // 8, lax.rem(ring // 2, 4), lax.rem(ring, 2)
    base = half * RING

    barrier = pltpu.get_barrier_semaphore()

    @pl.loop(1, RING)
    def _(k):
        peer = (base + lax.rem(ring + k, RING), group)
        pl.semaphore_signal(barrier, inc=1, device_id=peer, device_id_type=MESH)

    for part in range(2):
        peer = (part * RING + ring, 1 - group)
        pl.semaphore_signal(barrier, inc=1, device_id=peer, device_id_type=MESH)

    @pl.when(half == 1)
    def _():
        pl.semaphore_signal(barrier, inc=1, device_id=(ring, group), device_id_type=MESH)

    @pl.when(place > 0)
    def _():
        pl.semaphore_signal(barrier, inc=1, device_id=(place - 1, group), device_id_type=MESH)

    def tile_of(step):
        near = step + 1
        return lax.rem(x + near // 2, 4) * 2 + lax.rem(z // 2 + near, 2)

    def load(step, slot, part):
        lane = pl.multiple_of(tile_of(step) * LANES + part * 8 * LANES, LANES)
        return pltpu.make_async_copy(
            qkv_ref.at[:, :, pl.ds(lane, LANES)], raw.at[slot, part], load_sem.at[slot, part]
        )

    def column(part):
        lane = pl.multiple_of((ring // 4) * LANES + part * 8 * LANES, LANES)
        return pltpu.make_async_copy(
            filter_ref.at[:, pl.ds(lane, LANES)], columns.at[part], column_sem.at[part]
        )

    above_copy = pltpu.make_async_remote_copy(
        src_ref=qkv_ref.at[:, pl.ds(TOK - 8, 8)],
        dst_ref=above,
        send_sem=above_send,
        recv_sem=above_recv,
        device_id=(lax.rem(place + 1, shards), group),
        device_id_type=MESH,
    )

    for part in range(2):
        load(0, 0, part).start()
    for part in range(2):
        column(part).start()

    @pl.when(place == 0)
    def _():
        above[...] = jnp.zeros_like(above)

    fill_mask(doc_ref, mask_ref, half)

    expected = RING + 1 + jnp.where(half == 0, 1, 0)
    expected = expected + jnp.where(place < shards - 1, 1, 0)
    pl.semaphore_wait(barrier, expected)

    @pl.when(place < shards - 1)
    def _():
        above_copy.start()

    sources = (gated_ref, query_ref)

    def send(chunk, kind):
        for dx, dz, dc in displacements():
            to = (lax.rem(x + dx + 4, 4) * 4 + lax.rem(z + dz + 4, 4)) * 2 + lax.rem(core + dc, 2)
            pltpu.make_async_remote_copy(
                src_ref=sources[kind].at[chunk, to],
                dst_ref=got.at[chunk, kind, ring],
                send_sem=send_sem.at[chunk, kind],
                recv_sem=recv_sem.at[chunk, kind],
                device_id=(base + to, group),
                device_id_type=MESH,
            ).start()
        pltpu.make_async_copy(
            sources[kind].at[chunk, ring], got.at[chunk, kind, ring], recv_sem.at[chunk, kind]
        ).start()

    def send_tile(tile, chunk, kind):
        for member in range(4):
            to = tile * 4 + member

            @pl.when(to == ring)
            def _():
                pltpu.make_async_copy(
                    sources[kind].at[chunk, to], got.at[chunk, kind, to], recv_sem.at[chunk, kind]
                ).start()

            @pl.when(to != ring)
            def _():
                pltpu.make_async_remote_copy(
                    src_ref=sources[kind].at[chunk, to],
                    dst_ref=got.at[chunk, kind, ring],
                    send_sem=send_sem.at[chunk, kind],
                    recv_sem=recv_sem.at[chunk, kind],
                    device_id=(base + to, group),
                    device_id_type=MESH,
                ).start()

    def arrived(chunk, kind):
        pltpu.make_async_copy(
            sources[kind].at[chunk], got.at[chunk, kind], recv_sem.at[chunk, kind]
        ).wait()

    def edge_copy(chunk):
        return pltpu.make_async_remote_copy(
            src_ref=got.at[chunk, 0, pl.ds(RING - TAIL, TAIL)],
            dst_ref=edge.at[chunk],
            send_sem=edge_send.at[chunk],
            recv_sem=edge_recv.at[chunk],
            device_id=(RING + ring, group),
            device_id_type=MESH,
        )

    corner = half == group

    def span_of(piece, count=1):
        return pl.ds(piece * PIECE, PIECE * count)

    def turn(chunk, part, piece):
        span = span_of(piece)
        source = ready.at[chunk, part, span]

        @pl.when(jnp.logical_not(corner))
        def _():
            pltpu.make_async_remote_copy(
                src_ref=source,
                dst_ref=out_ref.at[group, chunk // 2, span, pl.ds(lax.rem(chunk, 2) * HALF, HALF)],
                send_sem=turn_send.at[chunk, part],
                recv_sem=turn_recv.at[0],
                device_id=(part * RING + ring, 1 - group),
                device_id_type=MESH,
            ).start()

        @pl.when(corner & (half == part))
        def _():
            pltpu.make_async_copy(
                source, out_ref.at[group, chunk // 2, span, pl.ds(lax.rem(chunk, 2) * HALF, HALF)], turn_recv.at[0]
            ).start()

        @pl.when(corner & (half != part))
        def _():
            pltpu.make_async_remote_copy(
                src_ref=source,
                dst_ref=relay.at[chunk, span],
                send_sem=turn_send.at[chunk, part],
                recv_sem=relay_recv.at[chunk, piece // LEG],
                device_id=(part * RING + ring, 1 - group),
                device_id_type=MESH,
            ).start()

    def forward(chunk):
        @pl.when(corner)
        def _():
            for leg in range(PIECES // LEG):
                span = span_of(leg * LEG, LEG)
                copy = pltpu.make_async_remote_copy(
                    src_ref=relay.at[chunk, span],
                    dst_ref=out_ref.at[1 - group, chunk // 2, span, pl.ds(lax.rem(chunk, 2) * HALF, HALF)],
                    send_sem=relay_send.at[chunk],
                    recv_sem=turn_recv.at[0],
                    device_id=(half * RING + ring, 1 - group),
                    device_id_type=MESH,
                )
                pltpu.make_async_copy(
                    ready.at[chunk, 0, span], relay.at[chunk, span], relay_recv.at[chunk, leg]
                ).wait()
                copy.start()

    doc_here = doc_ref[place]
    joined = (place > 0) & (doc_ref[jnp.maximum(place - 1, 0)] == doc_here)
    linked = jnp.where(joined, 1.0, 0.0).astype(jnp.float32)
    closing = (place == shards - 1) | (doc_ref[jnp.minimum(place + 1, shards - 1)] != doc_here)
    limit = jnp.where(closing, live_ref[place], TOK)

    for part in range(2):
        column(part).wait()
    fill_taps(columns, skip_ref, turned, taps_ref, direct_ref, ring)

    @pl.when(place > 0)
    def _():
        above_copy.wait_recv()

    @pl.loop(0, STEPS)
    def _(step):
        slot = lax.rem(step, 2)
        tile = tile_of(step)
        keep = jnp.where(
            lax.broadcasted_iota(jnp.int32, (TOK, LANES), 0) < limit, 1.0, 0.0
        ).astype(jnp.float32)

        @pl.when(step + 1 < STEPS)
        def _():
            for part in range(2):
                load(step + 1, 1 - slot, part).start()

        gates = []
        for part in range(2):
            load(step, slot, part).wait()
            lane = pl.multiple_of(tile * LANES + part * 8 * LANES, LANES)
            parts = [
                bordered(
                    raw[slot, part, a].astype(jnp.float32),
                    above[a, :, pl.ds(lane, LANES)].astype(jnp.float32)[6:8] * linked,
                    short_ref[a, :, pl.ds(lane, LANES)],
                )
                for a in range(3)
            ]
            query = parts[0].astype(jnp.bfloat16).astype(jnp.float32) * keep
            gates.append((parts[1] * parts[2] * keep, query))
        for which in range(2):
            for block in range(BLOCKS):
                rows = slice(block * LANES, (block + 1) * LANES)
                first = gates[0][which][rows].T
                second = gates[1][which][rows].T
                for peer in range(4):
                    for chunk in range(CHUNKS):
                        at = peer * 32 + chunk * HALF
                        both = jnp.concatenate(
                            [first[at : at + HALF], second[at : at + HALF]], axis=0
                        )
                        sources[which][chunk, tile * 4 + peer, block] = both.astype(jnp.bfloat16)
        send_tile(tile, 0, 0)
        send_tile(tile, 1, 0)

    send(0, 1)
    send(1, 1)

    @pl.loop(2, AHEAD)
    def _(chunk):
        send(chunk, 0)
        send(chunk, 1)


    def long_conv(chunk):
        @pl.loop(0, WIDTH // 2)
        def _(two):
            for i in range(2):
                channel = two * 2 + i
                fill_toeplitz(taps_ref, toep, chunk * WIDTH + channel, channel)

        arrived(chunk, 0)

        @pl.when(half == 0)
        def _():
            edge_copy(chunk).start()
            wide[pl.ds(0, SPAN * WIDTH)] = jnp.zeros((SPAN * WIDTH, LANES), jnp.float32)

        @pl.loop(0, RING)
        def _(shard):
            at = pl.multiple_of((SPAN + shard * BLOCKS) * WIDTH, 8)
            wide[pl.ds(at, BLOCKS * WIDTH)] = (
                got[chunk, 0, shard].reshape(BLOCKS * WIDTH, LANES).astype(jnp.float32)
            )

        @pl.when(half == 1)
        def _():
            edge_copy(chunk).wait_recv()
            for shard in range(TAIL):
                wide[shard * BLOCKS * WIDTH : (shard + 1) * BLOCKS * WIDTH] = (
                    edge[chunk, shard].reshape(BLOCKS * WIDTH, LANES).astype(jnp.float32)
                )

        @pl.loop(0, WIDTH // 4)
        def _(four):
            for i in range(4):
                channel = four * 4 + i
                convolve(wide, toep, mask_ref, total.at[lax.rem(chunk, 2)], channel, channel)

    def product(chunk):
        arrived(chunk, 1)
        direct = direct_ref[pl.ds(pl.multiple_of(chunk * WIDTH, WIDTH), WIDTH)]
        for piece in range(PIECES):
            @pl.loop(0, RING // PIECES)
            def _(offset):
                shard = piece * (RING // PIECES) + offset
                for block in range(BLOCKS):
                    row = shard * BLOCKS + block
                    at = pl.multiple_of(row * WIDTH, WIDTH)
                    gated = got[chunk, 0, shard, block].astype(jnp.float32)
                    query = got[chunk, 1, shard, block].astype(jnp.float32)
                    value = query * (total[lax.rem(chunk, 2), pl.ds(at, WIDTH)] + direct * gated)
                    ready[chunk, 0, row] = value[:HALF].astype(jnp.bfloat16)
                    ready[chunk, 1, row] = value[HALF:].astype(jnp.bfloat16)

            for part in range(2):
                turn(chunk, part, piece)

    @pl.loop(0, CHUNKS)
    def _(chunk):
        @pl.when(chunk + AHEAD < CHUNKS)
        def _():
            send(chunk + AHEAD, 0)
            send(chunk + AHEAD, 1)

        long_conv(chunk)
        product(chunk)

        @pl.when(chunk > 0)
        def _():
            forward(chunk - 1)

    forward(CHUNKS - 1)

    @pl.loop(0, CHUNKS)
    def _(chunk):
        for kind in range(2):
            pltpu.make_async_remote_copy(
                src_ref=sources[kind].at[chunk, pl.ds(0, RING - 1)],
                dst_ref=got.at[chunk, kind, pl.ds(0, RING - 1)],
                send_sem=send_sem.at[chunk, kind],
                recv_sem=recv_sem.at[chunk, kind],
                device_id=(place, group),
                device_id_type=MESH,
            ).wait_send()
        def drained(source, sem):
            pltpu.make_async_remote_copy(
                src_ref=source,
                dst_ref=source,
                send_sem=sem,
                recv_sem=turn_recv.at[0],
                device_id=(place, group),
                device_id_type=MESH,
            ).wait_send()

        for part in range(2):
            @pl.when(jnp.logical_not(corner & (half == part)))
            def _():
                drained(ready.at[chunk, part], turn_send.at[chunk, part])

        @pl.when(corner)
        def _():
            drained(relay.at[chunk], relay_send.at[chunk])

        @pl.when(half == 0)
        def _():
            edge_copy(chunk).wait_send()

    @pl.when(place < shards - 1)
    def _():
        above_copy.wait_send()

    pltpu.make_async_copy(out_ref, out_ref, turn_recv.at[0]).wait()


def local(qkv, short_filter, long_filter, skip, shard_doc, live):
    vmem = pl.BlockSpec(memory_space=pltpu.VMEM)
    smem = pl.BlockSpec(memory_space=pltpu.SMEM)
    hbm = pl.BlockSpec(memory_space=pl.ANY)
    dma = pltpu.SemaphoreType.DMA
    parcel = (CHUNKS, RING, BLOCKS, WIDTH, LANES)
    moved = pl.pallas_call(
        exchange_kernel,
        out_shape=jax.ShapeDtypeStruct((2, CHUNKS // 2, ROWS, WIDTH, LANES), jnp.bfloat16),
        in_specs=[smem, smem, hbm, vmem, hbm, vmem],
        out_specs=hbm,
        scratch_shapes=[
            pltpu.VMEM((2, 2, 3, TOK, LANES), jnp.bfloat16),
            pltpu.VMEM((3, 8, qkv.shape[2]), jnp.bfloat16),
            pltpu.VMEM(parcel, jnp.bfloat16),
            pltpu.VMEM(parcel, jnp.bfloat16),
            pltpu.VMEM((2, SPAN * LANES, LANES), jnp.bfloat16),
            pltpu.VMEM((LANES, LANES), jnp.float32),
            pltpu.VMEM((SPAN, CHUNKS * WIDTH, LANES), jnp.float32),
            pltpu.VMEM((CHUNKS * WIDTH, LANES), jnp.float32),
            pltpu.VMEM((LAGS, ROWS, LANES), jnp.bfloat16),
            pltpu.VMEM((CHUNKS, 2, RING, BLOCKS, WIDTH, LANES), jnp.bfloat16),
            pltpu.VMEM((CHUNKS, TAIL, BLOCKS, WIDTH, LANES), jnp.bfloat16),
            pltpu.VMEM(((SPAN + ROWS) * WIDTH, LANES), jnp.float32),
            pltpu.VMEM((2, ROWS * WIDTH, LANES), jnp.float32),
            pltpu.VMEM((CHUNKS, 2, ROWS, HALF, LANES), jnp.bfloat16),
            pltpu.VMEM((CHUNKS, ROWS, HALF, LANES), jnp.bfloat16),
            pltpu.VMEM((WIDTH, LAGS * LANES, LANES), jnp.bfloat16),
            dma((2, 2)),
            dma,
            dma,
            dma((2,)),
            dma((CHUNKS, 2)),
            dma((CHUNKS, 2)),
            dma((CHUNKS,)),
            dma((CHUNKS,)),
            dma((CHUNKS, 2)),
            dma((1,)),
            dma((CHUNKS,)),
            dma((CHUNKS, PIECES // LEG)),
        ],
        compiler_params=pltpu.CompilerParams(
            collective_id=0, has_side_effects=True, vmem_limit_bytes=60 * 2**20
        ),
    )(shard_doc, live, qkv, short_filter, long_filter, skip.reshape(-1, LANES))
    return moved.transpose(0, 1, 3, 2, 4).reshape(2, CHUNKS * HALF, ROWS * LANES)


def solution(mesh):
    return jax.shard_map(
        local,
        mesh=mesh,
        in_specs=(P(None, "ctx", "ch"), P(None, None, "ch"), P(None, "ch"), P("ch"), P(), P()),
        out_specs=P(None, "ctx", "ch"),
        check_vma=False,
    )
```

```python
import jax
import jax.numpy as jnp
from jax import lax
from jax.experimental import pallas as pl
from jax.experimental.pallas import tpu as pltpu
from jax.sharding import PartitionSpec as P

MESH = pl.DeviceIdType.MESH
LANES = 128
TOK = 512
BLOCKS = TOK // LANES
RING = 32
CHUNKS = 8
HALF = 4
WIDTH = 2 * HALF
SPAN = 16
ROWS = RING * BLOCKS
LAGS = SPAN + 1
TAIL = SPAN // BLOCKS
STEPS = 8
AHEAD = 4
PIECES = 4
LEG = 1
PIECE = ROWS // PIECES


def bordered(x, above, taps):
    place = lax.broadcasted_iota(jnp.int32, x.shape, 0)
    one = jnp.where(place == 0, above[1:2], pltpu.roll(x, 1, 0))
    two = jnp.where(place == 0, above[0:1], jnp.where(place == 1, above[1:2], pltpu.roll(x, 2, 0)))
    return taps[0:1] * x + taps[1:2] * one + taps[2:3] * two


def displacements():
    groups = [
        [(1, 1), (-1, -1), (1, -1), (-1, 1)],
        [(2, 1), (1, 2), (2, -1), (-1, 2)],
        [(1, 0), (0, 1), (-1, 0), (0, -1)],
        [(2, 2), (2, 0), (0, 2)],
    ]
    order = [(dx, dz, core) for core in (0, 1) for group in groups for dx, dz in group]
    return order + [(0, 0, 1)]


def fill_toeplitz(taps_ref, toep_ref, channel, slot):
    row = lax.broadcasted_iota(jnp.int32, (LANES, LANES), 0)
    col = lax.broadcasted_iota(jnp.int32, (LANES, LANES), 1)
    causal = col >= row
    older = jnp.zeros((LANES, LANES), jnp.bfloat16)
    for lag in range(LAGS):
        newer = jnp.zeros((LANES, LANES), jnp.bfloat16)
        if lag < SPAN:
            spread = jnp.broadcast_to(taps_ref[lag, pl.ds(channel, 1), :], (LANES, LANES))
            newer = pltpu.roll(spread, 0, 1, stride=1, stride_axis=0).astype(jnp.bfloat16)
        toep_ref[slot, lag * LANES : (lag + 1) * LANES] = jnp.where(causal, newer, older)
        older = newer


def convolve(wide_ref, toep_ref, mask_ref, total_ref, channel, slot):
    tiles = {
        u: wide_ref[pl.ds((SPAN + u) * WIDTH + channel, 16, stride=8 * WIDTH), :].astype(jnp.bfloat16)
        for u in range(-SPAN, 8)
    }
    columns = [
        jnp.concatenate([tiles[p - lag] for p in range(8)], axis=0) * mask_ref[lag]
        for lag in range(LAGS)
    ]
    left = jnp.concatenate(columns, axis=1)
    total = jnp.dot(left, toep_ref[slot], preferred_element_type=jnp.float32)
    for p in range(8):
        total_ref[pl.ds(p * WIDTH + channel, 16, stride=8 * WIDTH), :] = total[p * 16 : (p + 1) * 16]


def fill_mask(doc_ref, mask_ref, half):
    shape = (ROWS, LANES)
    index = lax.broadcasted_iota(jnp.int32, shape, 0)
    row = lax.rem(index, 16) * 8 + index // 16
    shard = row // BLOCKS + half * RING
    first = jnp.zeros(shape, jnp.int32)
    opened = jnp.int32(0)
    for spot in range(1, 2 * RING):
        opened = jnp.where(doc_ref[spot] != doc_ref[spot - 1], jnp.int32(spot), opened)
        first = jnp.where(shard == spot, opened, first)
    reach = row + half * ROWS - first * BLOCKS
    for lag in range(LAGS):
        mask_ref[lag] = jnp.where(reach >= lag, 1.0, 0.0).astype(jnp.bfloat16)


def fill_taps(columns, skip_ref, turned, taps_ref, direct_ref, ring):
    corner = lax.rem(ring, 4) * 32

    for part in range(2):
        @pl.loop(0, SPAN)
        def _(lag):
            at = pl.multiple_of(lag * LANES, LANES)
            turned[...] = columns[part, pl.ds(at, LANES), :].astype(jnp.float32).T
            for chunk in range(CHUNKS):
                to = chunk * WIDTH + part * HALF
                taps_ref[lag, to : to + HALF] = turned[pl.ds(pl.multiple_of(corner + chunk // 2 * 8, 8), 8)][chunk % 2 * HALF : chunk % 2 * HALF + HALF]

        line = skip_ref[pl.ds(part * 8 + ring // 4, 1), :]
        turned[...] = jnp.broadcast_to(line, (LANES, LANES)).T
        for chunk in range(CHUNKS):
            to = chunk * WIDTH + part * HALF
            direct_ref[to : to + HALF] = turned[pl.ds(pl.multiple_of(corner + chunk // 2 * 8, 8), 8)][chunk % 2 * HALF : chunk % 2 * HALF + HALF]


def exchange_kernel(
    doc_ref, live_ref, qkv_ref, short_ref, filter_ref, skip_ref, out_ref,
    raw, above, gated_ref, query_ref, columns, turned, taps_ref, direct_ref, mask_ref,
    got, edge, wide, total, ready, relay, toep,
    load_sem, above_send, above_recv, column_sem,
    send_sem, recv_sem, edge_send, edge_recv, turn_send, turn_recv, relay_send, relay_recv,
):
    place = lax.axis_index("ctx")
    group = lax.axis_index("ch")
    shards = lax.axis_size("ctx")
    half = place // RING
    ring = lax.rem(place, RING)
    x, z, core = ring // 8, lax.rem(ring // 2, 4), lax.rem(ring, 2)
    base = half * RING

    barrier = pltpu.get_barrier_semaphore()

    @pl.loop(1, RING)
    def _(k):
        peer = (base + lax.rem(ring + k, RING), group)
        pl.semaphore_signal(barrier, inc=1, device_id=peer, device_id_type=MESH)

    for part in range(2):
        peer = (part * RING + ring, 1 - group)
        pl.semaphore_signal(barrier, inc=1, device_id=peer, device_id_type=MESH)

    @pl.when(half == 1)
    def _():
        pl.semaphore_signal(barrier, inc=1, device_id=(ring, group), device_id_type=MESH)

    @pl.when(place > 0)
    def _():
        pl.semaphore_signal(barrier, inc=1, device_id=(place - 1, group), device_id_type=MESH)

    def tile_of(step):
        near = step + 1
        return lax.rem(x + near // 2, 4) * 2 + lax.rem(z // 2 + near, 2)

    def load(step, slot, part):
        lane = pl.multiple_of(tile_of(step) * LANES + part * 8 * LANES, LANES)
        return pltpu.make_async_copy(
            qkv_ref.at[:, :, pl.ds(lane, LANES)], raw.at[slot, part], load_sem.at[slot, part]
        )

    def column(part):
        lane = pl.multiple_of((ring // 4) * LANES + part * 8 * LANES, LANES)
        return pltpu.make_async_copy(
            filter_ref.at[:, pl.ds(lane, LANES)], columns.at[part], column_sem.at[part]
        )

    above_copy = pltpu.make_async_remote_copy(
        src_ref=qkv_ref.at[:, pl.ds(TOK - 8, 8)],
        dst_ref=above,
        send_sem=above_send,
        recv_sem=above_recv,
        device_id=(lax.rem(place + 1, shards), group),
        device_id_type=MESH,
    )

    for part in range(2):
        load(0, 0, part).start()
    for part in range(2):
        column(part).start()

    @pl.when(place == 0)
    def _():
        above[...] = jnp.zeros_like(above)

    fill_mask(doc_ref, mask_ref, half)

    expected = RING + 1 + jnp.where(half == 0, 1, 0)
    expected = expected + jnp.where(place < shards - 1, 1, 0)
    pl.semaphore_wait(barrier, expected)

    @pl.when(place < shards - 1)
    def _():
        above_copy.start()

    sources = (gated_ref, query_ref)

    def send(chunk, kind):
        for dx, dz, dc in displacements():
            to = (lax.rem(x + dx + 4, 4) * 4 + lax.rem(z + dz + 4, 4)) * 2 + lax.rem(core + dc, 2)
            pltpu.make_async_remote_copy(
                src_ref=sources[kind].at[chunk, to],
                dst_ref=got.at[chunk, kind, ring],
                send_sem=send_sem.at[chunk, kind],
                recv_sem=recv_sem.at[chunk, kind],
                device_id=(base + to, group),
                device_id_type=MESH,
            ).start()
        pltpu.make_async_copy(
            sources[kind].at[chunk, ring], got.at[chunk, kind, ring], recv_sem.at[chunk, kind]
        ).start()

    def send_tile(tile, chunk, kind):
        for member in range(4):
            to = tile * 4 + member

            @pl.when(to == ring)
            def _():
                pltpu.make_async_copy(
                    sources[kind].at[chunk, to], got.at[chunk, kind, to], recv_sem.at[chunk, kind]
                ).start()

            @pl.when(to != ring)
            def _():
                pltpu.make_async_remote_copy(
                    src_ref=sources[kind].at[chunk, to],
                    dst_ref=got.at[chunk, kind, ring],
                    send_sem=send_sem.at[chunk, kind],
                    recv_sem=recv_sem.at[chunk, kind],
                    device_id=(base + to, group),
                    device_id_type=MESH,
                ).start()

    def arrived(chunk, kind):
        pltpu.make_async_copy(
            sources[kind].at[chunk], got.at[chunk, kind], recv_sem.at[chunk, kind]
        ).wait()

    def edge_copy(chunk):
        return pltpu.make_async_remote_copy(
            src_ref=got.at[chunk, 0, pl.ds(RING - TAIL, TAIL)],
            dst_ref=edge.at[chunk],
            send_sem=edge_send.at[chunk],
            recv_sem=edge_recv.at[chunk],
            device_id=(RING + ring, group),
            device_id_type=MESH,
        )

    corner = half == group

    def span_of(piece, count=1):
        return pl.ds(piece * PIECE, PIECE * count)

    def turn(chunk, part, piece):
        span = span_of(piece)
        source = ready.at[chunk, part, span]

        @pl.when(jnp.logical_not(corner))
        def _():
            pltpu.make_async_remote_copy(
                src_ref=source,
                dst_ref=out_ref.at[group, chunk // 2, span, pl.ds(lax.rem(chunk, 2) * HALF, HALF)],
                send_sem=turn_send.at[chunk, part],
                recv_sem=turn_recv.at[0],
                device_id=(part * RING + ring, 1 - group),
                device_id_type=MESH,
            ).start()

        @pl.when(corner & (half == part))
        def _():
            pltpu.make_async_copy(
                source, out_ref.at[group, chunk // 2, span, pl.ds(lax.rem(chunk, 2) * HALF, HALF)], turn_recv.at[0]
            ).start()

        @pl.when(corner & (half != part))
        def _():
            pltpu.make_async_remote_copy(
                src_ref=source,
                dst_ref=relay.at[chunk, span],
                send_sem=turn_send.at[chunk, part],
                recv_sem=relay_recv.at[chunk, piece // LEG],
                device_id=(part * RING + ring, 1 - group),
                device_id_type=MESH,
            ).start()

    def forward(chunk):
        @pl.when(corner)
        def _():
            for leg in range(PIECES // LEG):
                span = span_of(leg * LEG, LEG)
                copy = pltpu.make_async_remote_copy(
                    src_ref=relay.at[chunk, span],
                    dst_ref=out_ref.at[1 - group, chunk // 2, span, pl.ds(lax.rem(chunk, 2) * HALF, HALF)],
                    send_sem=relay_send.at[chunk],
                    recv_sem=turn_recv.at[0],
                    device_id=(half * RING + ring, 1 - group),
                    device_id_type=MESH,
                )
                pltpu.make_async_copy(
                    ready.at[chunk, 0, span], relay.at[chunk, span], relay_recv.at[chunk, leg]
                ).wait()
                copy.start()

    doc_here = doc_ref[place]
    joined = (place > 0) & (doc_ref[jnp.maximum(place - 1, 0)] == doc_here)
    linked = jnp.where(joined, 1.0, 0.0).astype(jnp.float32)
    closing = (place == shards - 1) | (doc_ref[jnp.minimum(place + 1, shards - 1)] != doc_here)
    limit = jnp.where(closing, live_ref[place], TOK)

    for part in range(2):
        column(part).wait()
    fill_taps(columns, skip_ref, turned, taps_ref, direct_ref, ring)

    @pl.when(place > 0)
    def _():
        above_copy.wait_recv()

    @pl.loop(0, STEPS)
    def _(step):
        slot = lax.rem(step, 2)
        tile = tile_of(step)
        keep = jnp.where(
            lax.broadcasted_iota(jnp.int32, (TOK, LANES), 0) < limit, 1.0, 0.0
        ).astype(jnp.float32)

        @pl.when(step + 1 < STEPS)
        def _():
            for part in range(2):
                load(step + 1, 1 - slot, part).start()

        gates = []
        for part in range(2):
            load(step, slot, part).wait()
            lane = pl.multiple_of(tile * LANES + part * 8 * LANES, LANES)
            parts = [
                bordered(
                    raw[slot, part, a].astype(jnp.float32),
                    above[a, :, pl.ds(lane, LANES)].astype(jnp.float32)[6:8] * linked,
                    short_ref[a, :, pl.ds(lane, LANES)],
                )
                for a in range(3)
            ]
            query = parts[0].astype(jnp.bfloat16).astype(jnp.float32) * keep
            gates.append((parts[1] * parts[2] * keep, query))
        for which in range(2):
            for block in range(BLOCKS):
                rows = slice(block * LANES, (block + 1) * LANES)
                first = gates[0][which][rows].T
                second = gates[1][which][rows].T
                for peer in range(4):
                    for chunk in range(CHUNKS):
                        at = peer * 32 + chunk * HALF
                        both = jnp.concatenate(
                            [first[at : at + HALF], second[at : at + HALF]], axis=0
                        )
                        sources[which][chunk, tile * 4 + peer, block] = both.astype(jnp.bfloat16)
        send_tile(tile, 0, 0)
        send_tile(tile, 1, 0)

    send(0, 1)
    send(1, 1)

    @pl.loop(2, AHEAD)
    def _(chunk):
        send(chunk, 0)
        send(chunk, 1)


    def long_conv(chunk):
        @pl.loop(0, WIDTH // 2)
        def _(two):
            for i in range(2):
                channel = two * 2 + i
                fill_toeplitz(taps_ref, toep, chunk * WIDTH + channel, channel)

        arrived(chunk, 0)

        @pl.when(half == 0)
        def _():
            edge_copy(chunk).start()
            wide[pl.ds(0, SPAN * WIDTH)] = jnp.zeros((SPAN * WIDTH, LANES), jnp.float32)

        @pl.loop(0, RING)
        def _(shard):
            at = pl.multiple_of((SPAN + shard * BLOCKS) * WIDTH, 8)
            wide[pl.ds(at, BLOCKS * WIDTH)] = (
                got[chunk, 0, shard].reshape(BLOCKS * WIDTH, LANES).astype(jnp.float32)
            )

        @pl.when(half == 1)
        def _():
            edge_copy(chunk).wait_recv()
            for shard in range(TAIL):
                wide[shard * BLOCKS * WIDTH : (shard + 1) * BLOCKS * WIDTH] = (
                    edge[chunk, shard].reshape(BLOCKS * WIDTH, LANES).astype(jnp.float32)
                )

        @pl.loop(0, WIDTH // 8)
        def _(four):
            for i in range(8):
                channel = four * 8 + i
                convolve(wide, toep, mask_ref, total.at[lax.rem(chunk, 2)], channel, channel)

    def product(chunk):
        arrived(chunk, 1)
        direct = direct_ref[pl.ds(pl.multiple_of(chunk * WIDTH, WIDTH), WIDTH)]
        for piece in range(PIECES):
            @pl.loop(0, RING // PIECES)
            def _(offset):
                shard = piece * (RING // PIECES) + offset
                for block in range(BLOCKS):
                    row = shard * BLOCKS + block
                    at = pl.multiple_of(row * WIDTH, WIDTH)
                    gated = got[chunk, 0, shard, block].astype(jnp.float32)
                    query = got[chunk, 1, shard, block].astype(jnp.float32)
                    value = query * (total[lax.rem(chunk, 2), pl.ds(at, WIDTH)] + direct * gated)
                    ready[chunk, 0, row] = value[:HALF].astype(jnp.bfloat16)
                    ready[chunk, 1, row] = value[HALF:].astype(jnp.bfloat16)

            for part in range(2):
                turn(chunk, part, piece)

    @pl.loop(0, CHUNKS)
    def _(chunk):
        @pl.when(chunk + AHEAD < CHUNKS)
        def _():
            send(chunk + AHEAD, 0)
            send(chunk + AHEAD, 1)

        long_conv(chunk)
        product(chunk)

        @pl.when(chunk > 0)
        def _():
            forward(chunk - 1)

    forward(CHUNKS - 1)

    @pl.loop(0, CHUNKS)
    def _(chunk):
        for kind in range(2):
            pltpu.make_async_remote_copy(
                src_ref=sources[kind].at[chunk, pl.ds(0, RING - 1)],
                dst_ref=got.at[chunk, kind, pl.ds(0, RING - 1)],
                send_sem=send_sem.at[chunk, kind],
                recv_sem=recv_sem.at[chunk, kind],
                device_id=(place, group),
                device_id_type=MESH,
            ).wait_send()
        def drained(source, sem):
            pltpu.make_async_remote_copy(
                src_ref=source,
                dst_ref=source,
                send_sem=sem,
                recv_sem=turn_recv.at[0],
                device_id=(place, group),
                device_id_type=MESH,
            ).wait_send()

        for part in range(2):
            @pl.when(jnp.logical_not(corner & (half == part)))
            def _():
                drained(ready.at[chunk, part], turn_send.at[chunk, part])

        @pl.when(corner)
        def _():
            drained(relay.at[chunk], relay_send.at[chunk])

        @pl.when(half == 0)
        def _():
            edge_copy(chunk).wait_send()

    @pl.when(place < shards - 1)
    def _():
        above_copy.wait_send()

    pltpu.make_async_copy(out_ref, out_ref, turn_recv.at[0]).wait()


def local(qkv, short_filter, long_filter, skip, shard_doc, live):
    vmem = pl.BlockSpec(memory_space=pltpu.VMEM)
    smem = pl.BlockSpec(memory_space=pltpu.SMEM)
    hbm = pl.BlockSpec(memory_space=pl.ANY)
    dma = pltpu.SemaphoreType.DMA
    parcel = (CHUNKS, RING, BLOCKS, WIDTH, LANES)
    moved = pl.pallas_call(
        exchange_kernel,
        out_shape=jax.ShapeDtypeStruct((2, CHUNKS // 2, ROWS, WIDTH, LANES), jnp.bfloat16),
        in_specs=[smem, smem, hbm, vmem, hbm, vmem],
        out_specs=hbm,
        scratch_shapes=[
            pltpu.VMEM((2, 2, 3, TOK, LANES), jnp.bfloat16),
            pltpu.VMEM((3, 8, qkv.shape[2]), jnp.bfloat16),
            pltpu.VMEM(parcel, jnp.bfloat16),
            pltpu.VMEM(parcel, jnp.bfloat16),
            pltpu.VMEM((2, SPAN * LANES, LANES), jnp.bfloat16),
            pltpu.VMEM((LANES, LANES), jnp.float32),
            pltpu.VMEM((SPAN, CHUNKS * WIDTH, LANES), jnp.float32),
            pltpu.VMEM((CHUNKS * WIDTH, LANES), jnp.float32),
            pltpu.VMEM((LAGS, ROWS, LANES), jnp.bfloat16),
            pltpu.VMEM((CHUNKS, 2, RING, BLOCKS, WIDTH, LANES), jnp.bfloat16),
            pltpu.VMEM((CHUNKS, TAIL, BLOCKS, WIDTH, LANES), jnp.bfloat16),
            pltpu.VMEM(((SPAN + ROWS) * WIDTH, LANES), jnp.float32),
            pltpu.VMEM((2, ROWS * WIDTH, LANES), jnp.float32),
            pltpu.VMEM((CHUNKS, 2, ROWS, HALF, LANES), jnp.bfloat16),
            pltpu.VMEM((CHUNKS, ROWS, HALF, LANES), jnp.bfloat16),
            pltpu.VMEM((WIDTH, LAGS * LANES, LANES), jnp.bfloat16),
            dma((2, 2)),
            dma,
            dma,
            dma((2,)),
            dma((CHUNKS, 2)),
            dma((CHUNKS, 2)),
            dma((CHUNKS,)),
            dma((CHUNKS,)),
            dma((CHUNKS, 2)),
            dma((1,)),
            dma((CHUNKS,)),
            dma((CHUNKS, PIECES // LEG)),
        ],
        compiler_params=pltpu.CompilerParams(
            collective_id=0, has_side_effects=True, vmem_limit_bytes=60 * 2**20
        ),
    )(shard_doc, live, qkv, short_filter, long_filter, skip.reshape(-1, LANES))
    return moved.transpose(0, 1, 3, 2, 4).reshape(2, CHUNKS * HALF, ROWS * LANES)


def solution(mesh):
    return jax.shard_map(
        local,
        mesh=mesh,
        in_specs=(P(None, "ctx", "ch"), P(None, None, "ch"), P(None, "ch"), P("ch"), P(), P()),
        out_specs=P(None, "ctx", "ch"),
        check_vma=False,
    )
```
